512 devices in a mesh: gx: 8 (over y), gy: 4 (over z_lo, core), gz: 16 (over x, z_hi).
Axes of the slice: x: 4, y: 8, z: 8 (z_hi: 4, z_lo: 2; z = z_hi * 2 + z_lo), core: 2. Of those that a mesh axis runs over, the one named last changes fastest.
Arguments:
- features: bfloat16 [393216, 256], P(('gx', 'gy', 'gz')), may hold values from -6 to 6
- tile_values: bfloat16 [7168, 8, 128, 128], P(('gx', 'gy', 'gz')), as said below
- tile_columns: int32 [7168, 8], P(('gx', 'gy', 'gz')), may hold values from 0 to 13
- tile_present: int32 [7168, 8], P(('gx', 'gy', 'gz')), may hold values 0 or 1
- host_root: int32 [4096], P(('gx', 'gy')), may hold values from 0 to 15, as said below
- host_block: int32 [4096], P(('gx', 'gy')), may hold values from 0 to 1
- self_one: bfloat16 [256, 256], replicated, may hold values from -0.375 to 0.375
- neigh_one: bfloat16 [256, 256], replicated, may hold values from -0.375 to 0.375
- scale_one: float32 [256], replicated, may hold values from 0.25 to 1.75
- shift_one: float32 [256], replicated, may hold values from -3 to 3
- self_two: bfloat16 [256, 256], replicated, may hold values from -0.375 to 0.375
- neigh_two: bfloat16 [256, 256], replicated, may hold values from -0.375 to 0.375
Outputs:
- embedding: bfloat16 [393216, 256], P(('gx', 'gy', 'gz'))
The draws below stay inside these ranges and needn't reach their ends.
Inputs may be any that keep to these rules, and one draw needn't show every extreme that they name: `host_root`: never the holder's own gz index; the 8 replica slots of one device name 8 different devices. `tile_values`: entries lie in 0 to 1.8 / sqrt(1024).
All inputs are finite; a program needn't handle non-finite values. No bound on the sum of `tile_present` on one device may be relied on, other than what follows from the above.
Results may differ from the reference program's by a relative error of at most 0.012.
Values may be sent and summed in bfloat16 or wider, within the bound.
No kernel may reach another device: no remote copies, remote signals or barrier semaphores. Data moves between devices by JAX's collectives and lax.ppermute only.
A program may use at most 64 MiB of HBM per device.

```python
import math
import jax
import jax.numpy as jnp
from jax import lax

F = 256
TILE = 128
K = 8
OWN = 4
SPLIT = 2
HOST = 8
SLOTS = 14
VERTICES = 393216
N_GZ = 16
DEVICES = 512


def draw_tile_values(key, part):
    shape = (DEVICES * (OWN + SPLIT + HOST), K, TILE, TILE)
    present = jax.random.uniform(jax.random.fold_in(key, 1), shape) < 0.4
    size = jax.random.uniform(jax.random.fold_in(key, 2), shape, minval=0.5, maxval=1.5)
    values = jnp.where(present, size, 0.0) * (1.2 / math.sqrt(K * TILE))
    return values.astype(jnp.float32).astype(jnp.bfloat16)


def host_tables(key):
    scores = jax.random.randint(jax.random.fold_in(key, 11), (DEVICES, N_GZ - 1), 0, 1 << 20)
    scores = scores * N_GZ + jnp.arange(N_GZ - 1, dtype=jnp.int32)[None, :]
    picked = jnp.argsort(scores, axis=1)[:, :HOST].astype(jnp.int32)
    own = (jnp.arange(DEVICES, dtype=jnp.int32) % N_GZ)[:, None]
    roots = (own + 1 + picked) % N_GZ
    blocks = jax.random.randint(jax.random.fold_in(key, 12), (DEVICES, HOST), 0, SPLIT)
    return (roots.reshape(-1).astype(jnp.int32), blocks.reshape(-1).astype(jnp.int32))


def draw_host_root(key, part):
    return host_tables(key)[0]


def draw_host_block(key, part):
    return host_tables(key)[1]


def set_ends(drawn, rng, least, high):
    longest = drawn.shape.index(max(drawn.shape))
    spots = []
    for shift in (0, 1):
        where = [jax.random.randint(jax.random.fold_in(rng, axis), (), 0, length) for axis, length in enumerate(drawn.shape)]
        where[longest] = (where[longest] + shift) % drawn.shape[longest]
        spots.append(tuple(where))
    return drawn.at[spots[0]].set(least).at[spots[1]].set(high)


def steps_of(rng, dims, split, smallest, high):
    gain, own = 1.0, jax.random.fold_in(rng, 6)
    for axis_at, blocks in split:
        draws = jnp.exp(jax.random.uniform(jax.random.fold_in(own, axis_at), (blocks,), jnp.float32, smallest / len(split), high / len(split)))
        gain = gain * jnp.repeat(draws, dims[axis_at] // blocks).reshape([-1 if axis == axis_at else 1 for axis in range(len(dims))])
    return gain


def gaussian(rng, extent, deviation, reach, split=(), kind=jnp.bfloat16):
    array = deviation * jax.random.normal(rng, extent, jnp.float32)
    if split:
        array = array * steps_of(rng, extent, split, -0.22, 0.18)
    return jnp.clip(array, -reach, reach).astype(kind)


def setup_inputs(seed: int = 0) -> dict:
    seeds = jax.random.split(jax.random.key(seed), 13)
    return {
        "features": gaussian(seeds[0], (VERTICES, F), 1.0, 6.0, ((0, 512),)),
        "tile_values": draw_tile_values(jax.random.fold_in(seeds[12], 71), 0),
        "tile_columns": set_ends(jax.random.randint(seeds[2], (DEVICES * SLOTS, K), 0, SLOTS), jax.random.fold_in(seeds[2], 1), 0, SLOTS - 1).astype(jnp.int32),
        "tile_present": set_ends((jax.random.randint(seeds[3], (DEVICES * SLOTS, K), 0, 4) < 3).astype(jnp.int32), jax.random.fold_in(seeds[3], 1), 0, 1),
        "host_root": draw_host_root(jax.random.fold_in(seeds[12], 71), 0),
        "host_block": draw_host_block(jax.random.fold_in(seeds[12], 71), 0),
        "self_one": gaussian(seeds[6], (F, F), F ** -0.5, 0.375),
        "neigh_one": gaussian(seeds[7], (F, F), F ** -0.5, 0.375),
        "scale_one": jnp.clip(1.0 + 0.15 * jax.random.normal(seeds[8], (F,), jnp.float32), 0.25, 1.75),
        "shift_one": gaussian(seeds[9], (F,), 0.5, 3.0, (), jnp.float32),
        "self_two": gaussian(seeds[10], (F, F), F ** -0.5, 0.375),
        "neigh_two": gaussian(seeds[11], (F, F), F ** -0.5, 0.375),
    }


def aggregate(view, tile_values, tile_columns, tile_present):

    def one_device(items):
        held, tiles, columns, present = items
        picked = held[columns]
        picked = jnp.where(present[:, :, None, None] > 0, picked, jnp.zeros_like(picked))
        return jnp.einsum('bkij,bkjf->bif', tiles.astype(jnp.float32), picked.astype(jnp.float32))
    return lax.map(one_device, (view, tile_values, tile_columns, tile_present))

def layer(rows, tile_values, tile_columns, tile_present, host_root, host_block, w_self, w_neigh):
    rooted = rows.reshape(DEVICES, OWN + SPLIT, TILE, F)
    sender = jnp.repeat(jnp.arange(DEVICES, dtype=jnp.int32), HOST)
    base = sender // N_GZ * N_GZ
    source = ((base + host_root) * (OWN + SPLIT) + OWN + host_block).astype(jnp.int32)
    hosted = rows.reshape(DEVICES * (OWN + SPLIT), TILE, F)[source].reshape(DEVICES, HOST, TILE, F)
    view = jnp.concatenate([rooted, hosted], axis=1)
    tiles = tile_values.reshape(DEVICES, OWN + SPLIT + HOST, K, TILE, TILE)
    columns = tile_columns.reshape(DEVICES, OWN + SPLIT + HOST, K)
    present = tile_present.reshape(DEVICES, OWN + SPLIT + HOST, K)
    partial_value = aggregate(view, tiles, columns, present)
    sent = partial_value[:, OWN + SPLIT:].astype(jnp.bfloat16)
    sent = lax.optimization_barrier(sent).astype(jnp.float32).reshape(DEVICES * HOST, TILE, F)
    target = ((base + host_root) * SPLIT + host_block).astype(jnp.int32)
    remote = jax.ops.segment_sum(sent, target, num_segments=DEVICES * SPLIT).reshape(DEVICES, SPLIT, TILE, F)
    total = partial_value[:, :OWN + SPLIT].at[:, OWN:].add(remote)
    neighbours = total.astype(jnp.bfloat16).reshape(-1, F)
    return jnp.dot(rows, w_self, preferred_element_type=jnp.float32) + jnp.dot(neighbours, w_neigh, preferred_element_type=jnp.float32)

def reference(features, tile_values, tile_columns, tile_present, host_root, host_block, self_one, neigh_one, scale_one, shift_one, self_two, neigh_two):
    first = layer(features, tile_values, tile_columns, tile_present, host_root, host_block, self_one, neigh_one)
    count = first.shape[0]
    mean = lax.optimization_barrier(jnp.sum(first, axis=0)) / count
    meansq = lax.optimization_barrier(jnp.sum(first * first, axis=0)) / count
    var = meansq - mean * mean
    hidden = jax.nn.relu((first - mean) * lax.rsqrt(var + 1e-05) * scale_one + shift_one).astype(jnp.bfloat16)
    second = layer(hidden, tile_values, tile_columns, tile_present, host_root, host_block, self_two, neigh_two)
    return second.astype(jnp.bfloat16)
```

```python
import functools

import jax
import jax.numpy as jnp
from jax import lax
from jax.experimental import pallas as pl
from jax.experimental.pallas import tpu as pltpu
from jax.sharding import Mesh
from jax.sharding import PartitionSpec as P

OWN = 4
SPLIT = 2
ROOTED = 6
HOST = 8
SLOTS = 14
K = 8
TILE = 128
F = 256
GROUP = 16
CENTER_ROWS = 16
VMEM_BYTES = 12 << 20
GZ = ("gz_0", "gz_1")
GX_GY_GZ = ("gx", "gy_0", "gy_1", "gz_0", "gz_1")
GX_GY = ("gx", "gy_0", "gy_1")

f32 = jnp.float32
bf16 = jnp.bfloat16

ANY = pl.BlockSpec(memory_space=pl.ANY)
VMEM = pl.BlockSpec(memory_space=pltpu.VMEM)
SMEM = pl.BlockSpec(memory_space=pltpu.SMEM)
DMA = pltpu.SemaphoreType.DMA


def shape(dims, dtype):
    return jax.ShapeDtypeStruct(dims, dtype)


def call(body, name, flops, size, **kw):
    return pl.pallas_call(
        body,
        name=name,
        compiler_params=pltpu.CompilerParams(vmem_limit_bytes=VMEM_BYTES),
        cost_estimate=pl.CostEstimate(flops=flops, bytes_accessed=size, transcendentals=0),
        **kw,
    )


def dot(a, b):
    return jnp.dot(a, b, preferred_element_type=f32)


def my_place():
    return lax.axis_index("gz_0") * 4 + lax.axis_index("gz_1")


def send_selected(sel, blocks, out, sems):
    copies = [
        pltpu.make_async_copy(blocks.at[jnp.maximum(sel(q) - 1, 0)], out.at[q], sems.at[q])
        for q in range(GROUP)
    ]
    for c in copies:
        c.start()
    for c in copies:
        c.wait()


def outgoing_kernel(root, block, rows, out, sel, split, sem, sems):
    load = pltpu.make_async_copy(rows.at[pl.ds(OWN, SPLIT)], split, sem)
    load.start()
    mine = my_place()
    for q in range(GROUP):
        held = jnp.int32(0)
        for j in range(HOST):
            held = jnp.where(root[q * HOST + j] == mine, block[q * HOST + j] + 1, held)
        sel[q] = held
    load.wait()
    send_selected(lambda q: sel[q], split, out, sems)


def tile_row(cols, present, b, tiles, view):
    acc = None
    for k in range(K):
        slot = jnp.where(present[b, k] > 0, cols[b, k], SLOTS)
        term = dot(tiles[k], view[slot])
        acc = term if acc is None else acc + term
    return acc


def replica_rows(root, cols, present, tiles, out, view, tbuf, obuf, tsem, osem):
    mine = my_place()

    def send(h):
        return pltpu.make_async_copy(obuf.at[h], out.at[root[mine * HOST + h]], osem.at[h])

    def step(h, carry):
        pltpu.make_async_copy(tiles.at[ROOTED + h], tbuf.at[h], tsem.at[h]).wait()
        obuf[h] = tile_row(cols, present, ROOTED + h, tbuf.at[h], view).astype(bf16)

        @pl.when(h > 0)
        def _():
            send(h - 1).start()

        return carry

    lax.fori_loop(0, HOST, step, 0)
    send(HOST - 1).start()
    lax.fori_loop(0, HOST, lambda h, c: (send(h).wait(), c)[1], 0)


def load_tiles(tiles, first, count, tbuf, tsem):
    def step(i, carry):
        pltpu.make_async_copy(tiles.at[first + i], tbuf.at[i], tsem.at[i]).start()
        return carry

    lax.fori_loop(0, count, step, 0)


def load_view(root, rows, incoming, view, vsem):
    mine = my_place()
    copies = [pltpu.make_async_copy(rows, view.at[pl.ds(0, ROOTED)], vsem.at[0])]
    for h in range(HOST):
        copies.append(
            pltpu.make_async_copy(
                incoming.at[root[mine * HOST + h]], view.at[ROOTED + h], vsem.at[1 + h]
            )
        )
    for c in copies:
        c.start()
    return copies


def replica_kernel(root, cols, present, rows, incoming, tiles, out, view, tbuf, obuf, vsem, tsem, osem):
    copies = load_view(root, rows, incoming, view, vsem)
    load_tiles(tiles, ROOTED, HOST, tbuf, tsem)
    view[SLOTS] = jnp.zeros((TILE, F), bf16)
    for c in copies:
        c.wait()
    replica_rows(root, cols, present, tiles, out, view, tbuf, obuf, tsem, osem)


def own_kernel(
    root, cols, present, rows, incoming, tiles, w_self, w_neigh,
    first_own, self_split, part_split, sums, view, tbuf, vsem, tsem,
):
    copies = load_view(root, rows, incoming, view, vsem)
    load_tiles(tiles, 0, ROOTED, tbuf, tsem)
    view[SLOTS] = jnp.zeros((TILE, F), bf16)
    sums[...] = jnp.zeros((2, F), f32)
    for c in copies:
        c.wait()

    def partial(b):
        pltpu.make_async_copy(tiles.at[b], tbuf.at[b], tsem.at[b]).wait()
        return tile_row(cols, present, b, tbuf.at[b], view)

    def own(b, carry):
        neighbours = partial(b).astype(bf16)
        first = dot(view[b], w_self[...]) + dot(neighbours, w_neigh[...])
        first_own[b] = first
        sums[0:1] += jnp.sum(first, axis=0, keepdims=True)
        sums[1:2] += jnp.sum(first * first, axis=0, keepdims=True)
        return carry

    def split(s, carry):
        part_split[s] = partial(OWN + s)
        self_split[s] = dot(view[OWN + s], w_self[...])
        return carry

    lax.fori_loop(0, OWN, own, 0)
    lax.fori_loop(0, SPLIT, split, 0)


def add_replicas(sel, incoming, total):
    for q in range(GROUP):
        s = sel[q]

        @pl.when(s > 0)
        def _(q=q, s=s):
            total[s - 1] += incoming[q].astype(f32)


def split_kernel(sel, incoming, part_split, self_split, own_sums, w_neigh, first_split, out, sums, total, pay, sems):
    total[...] = part_split[...]
    add_replicas(sel, incoming, total)
    all_sums = own_sums[...]
    firsts = []
    for s in range(SPLIT):
        first = self_split[s] + dot(total[s].astype(bf16), w_neigh[...])
        first_split[s] = first
        firsts.append(first)
    s1, s2 = all_sums[0:1], all_sums[1:2]
    for first in firsts:
        s1 += jnp.sum(first, axis=0, keepdims=True)
        s2 += jnp.sum(first * first, axis=0, keepdims=True)
    sums[0:1] = s1
    sums[1:2] = s2
    center = (s1 * (1.0 / (ROOTED * TILE))).astype(bf16)
    shift = center.astype(f32)
    for s in range(SPLIT):
        pay[s, pl.ds(0, TILE)] = (firsts[s] - shift).astype(bf16)
        pay[s, pl.ds(TILE, CENTER_ROWS)] = jnp.broadcast_to(center, (CENTER_ROWS, F))
    send_selected(lambda q: sel[q], pay, out, sems)


def hidden_kernel(
    count, root, cols, present, sums, scale, shift, first_own, first_split, incoming, tiles,
    out, hidden, view, tbuf, obuf, tsem, osem, hsem,
):
    load_tiles(tiles, ROOTED, HOST, tbuf, tsem)
    mine = my_place()
    mean = sums[0:1] * (1.0 / count)
    var = sums[1:2] * (1.0 / count) - mean * mean
    inv = lax.rsqrt(var + 1e-5)

    def norm(first, less):
        return jax.nn.relu((first - less) * inv * scale[...] + shift[...]).astype(bf16)

    def own(b, carry):
        view[b] = norm(first_own[b], mean)
        return carry

    def split(s, carry):
        view[OWN + s] = norm(first_split[s], mean)
        return carry

    def hosted(h, carry):
        q = root[mine * HOST + h]
        centered = incoming[q, pl.ds(0, TILE)].astype(f32)
        center = incoming[q, pl.ds(TILE, CENTER_ROWS)].astype(f32)[0:1]
        view[ROOTED + h] = norm(centered, mean - center)
        return carry

    lax.fori_loop(0, OWN, own, 0)
    lax.fori_loop(0, SPLIT, split, 0)
    lax.fori_loop(0, HOST, hosted, 0)
    view[SLOTS] = jnp.zeros((TILE, F), bf16)
    replica_rows(root, cols, present, tiles, out, view, tbuf, obuf, tsem, osem)
    keep = pltpu.make_async_copy(view, hidden, hsem)
    keep.start()
    keep.wait()


def own_two_kernel(cols, present, hidden, tiles, w_self, w_neigh, out, self_split, part_split, view, tbuf, vsem, tsem):
    load = pltpu.make_async_copy(hidden, view, vsem)
    load.start()
    load_tiles(tiles, 0, ROOTED, tbuf, tsem)
    load.wait()

    def partial(b):
        pltpu.make_async_copy(tiles.at[b], tbuf.at[b], tsem.at[b]).wait()
        return tile_row(cols, present, b, tbuf.at[b], view)

    def own(b, carry):
        neighbours = partial(b).astype(bf16)
        second = dot(view[b], w_self[...]) + dot(neighbours, w_neigh[...])
        out[b] = second.astype(bf16)
        return carry

    def split(s, carry):
        part_split[s] = partial(OWN + s)
        self_split[s] = dot(view[OWN + s], w_self[...])
        return carry

    lax.fori_loop(0, OWN, own, 0)
    lax.fori_loop(0, SPLIT, split, 0)


def last_kernel(sel, incoming, part_split, self_split, w_neigh, begun, out, total, done, sem):
    total[...] = part_split[...]
    add_replicas(sel, incoming, total)
    for s in range(SPLIT):
        done[s] = (self_split[s] + dot(total[s].astype(bf16), w_neigh[...])).astype(bf16)
    put = pltpu.make_async_copy(done, out.at[pl.ds(OWN, SPLIT)], sem)
    put.start()
    put.wait()


MAC = 2 * TILE * TILE * F


def per_device(
    features, tile_values, tile_columns, tile_present, host_root, host_block,
    self_one, neigh_one, scale_one, shift_one, self_two, neigh_two,
):
    rows = features.reshape(ROOTED, TILE, F)
    scale, shift = scale_one.reshape(1, F), shift_one.reshape(1, F)
    count = features.shape[0] * lax.axis_size(GX_GY_GZ)
    wire = shape((GROUP, TILE, F), bf16)
    split_f32 = shape((SPLIT, TILE, F), f32)

    def exchange(blocks):
        return lax.all_to_all(blocks, GZ, split_axis=0, concat_axis=0, tiled=True)

    view_scratch = pltpu.VMEM((SLOTS + 1, TILE, F), bf16)

    def tile_scratch(n):
        return pltpu.VMEM((n, K, TILE, TILE), bf16)

    outgoing, sel = call(
        outgoing_kernel, "outgoing", 0, 2 << 20,
        out_shape=(wire, shape((GROUP,), jnp.int32)),
        in_specs=[SMEM, SMEM, ANY],
        out_specs=(ANY, SMEM),
        scratch_shapes=[pltpu.VMEM((SPLIT, TILE, F), bf16), DMA, DMA((GROUP,))],
    )(host_root, host_block, rows)
    incoming = exchange(outgoing)

    outgoing = call(
        replica_kernel, "replicas", 64 * MAC, 4 << 20,
        out_shape=wire,
        in_specs=[SMEM] * 3 + [ANY] * 3,
        out_specs=ANY,
        scratch_shapes=[
            view_scratch, tile_scratch(HOST), pltpu.VMEM((HOST, TILE, F), bf16),
            DMA((1 + HOST,)), DMA((HOST,)), DMA((HOST,)),
        ],
    )(host_root, tile_columns, tile_present, rows, incoming, tile_values)
    returned = exchange(outgoing)

    first_own, self_split, part_split, own_sums = call(
        own_kernel, "own_rows", 60 * MAC, 5 << 20,
        out_shape=(shape((OWN, TILE, F), f32), split_f32, split_f32, shape((2, F), f32)),
        in_specs=[SMEM] * 3 + [ANY] * 3 + [VMEM] * 2,
        out_specs=(VMEM,) * 4,
        scratch_shapes=[view_scratch, tile_scratch(ROOTED), DMA((1 + HOST,)), DMA((ROOTED,))],
    )(host_root, tile_columns, tile_present, rows, incoming, tile_values, self_one, neigh_one)

    first_split, outgoing, sums = call(
        split_kernel, "split_rows", 4 * MAC, 3 << 20,
        out_shape=(split_f32, shape((GROUP, TILE + CENTER_ROWS, F), bf16), shape((2, F), f32)),
        in_specs=[SMEM] + [VMEM] * 5,
        out_specs=(VMEM, ANY, VMEM),
        scratch_shapes=[
            pltpu.VMEM((SPLIT, TILE, F), f32),
            pltpu.VMEM((SPLIT, TILE + CENTER_ROWS, F), bf16),
            DMA((GROUP,)),
        ],
    )(sel, returned, part_split, self_split, own_sums, neigh_one)
    incoming = exchange(outgoing)
    for axes in (("gy_0", "gy_1"), "gz_0", "gz_1", "gx"):
        sums = lax.psum(sums, axes)

    outgoing, hidden = call(
        functools.partial(hidden_kernel, count), "hidden_replicas", 64 * MAC, 5 << 20,
        out_shape=(wire, shape((SLOTS + 1, TILE, F), bf16)),
        in_specs=[SMEM] * 3 + [VMEM] * 6 + [ANY],
        out_specs=(ANY, ANY),
        scratch_shapes=[
            view_scratch, tile_scratch(HOST), pltpu.VMEM((HOST, TILE, F), bf16),
            DMA((HOST,)), DMA((HOST,)), DMA,
        ],
    )(
        host_root, tile_columns, tile_present, sums, scale, shift,
        first_own, first_split, incoming, tile_values,
    )
    returned = exchange(outgoing)

    begun, self_split, part_split = call(
        own_two_kernel, "own_rows_two", 60 * MAC, 5 << 20,
        out_shape=(shape((ROOTED, TILE, F), bf16), split_f32, split_f32),
        in_specs=[SMEM] * 2 + [ANY] * 2 + [VMEM] * 2,
        out_specs=(VMEM,) * 3,
        scratch_shapes=[view_scratch, tile_scratch(ROOTED), DMA, DMA((ROOTED,))],
    )(tile_columns, tile_present, hidden, tile_values, self_two, neigh_two)

    embedding = call(
        last_kernel, "split_rows_two", 4 * MAC, 3 << 20,
        out_shape=shape((ROOTED, TILE, F), bf16),
        in_specs=[SMEM] + [VMEM] * 4 + [ANY],
        out_specs=ANY,
        input_output_aliases={5: 0},
        scratch_shapes=[pltpu.VMEM((SPLIT, TILE, F), f32), pltpu.VMEM((SPLIT, TILE, F), bf16), DMA],
    )(sel, returned, part_split, self_split, neigh_two, begun)
    return embedding.reshape(ROOTED * TILE, F)


def solution(mesh):
    finer = Mesh(
        mesh.devices.reshape(mesh.shape["gx"], 2, 2, 4, 4), ("gx", "gy_0", "gy_1", "gz_0", "gz_1")
    )
    return jax.shard_map(
        per_device,
        mesh=finer,
        in_specs=(
            P(GX_GY_GZ, None),
            P(GX_GY_GZ, None, None, None),
            P(GX_GY_GZ, None),
            P(GX_GY_GZ, None),
            P(GX_GY),
            P(GX_GY),
            P(),
            P(),
            P(),
            P(),
            P(),
            P(),
        ),
        out_specs=P(GX_GY_GZ, None),
        check_vma=False,
    )
```

```python
import functools

import jax
import jax.numpy as jnp
from jax import lax
from jax.experimental import pallas as pl
from jax.experimental.pallas import tpu as pltpu
from jax.sharding import Mesh
from jax.sharding import PartitionSpec as P

OWN = 4
SPLIT = 2
ROOTED = 6
HOST = 8
SLOTS = 14
K = 8
TILE = 128
F = 256
GROUP = 16
CENTER_ROWS = 16
VMEM_BYTES = 50 << 20
GZ = ("gz_0", "gz_1")
GX_GY_GZ = ("gx", "gy_0", "gy_1", "gz_0", "gz_1")
GX_GY = ("gx", "gy_0", "gy_1")
REST = ("gy_0", "gz_0", "gz_1")
ROOTS_AT = 112
SEL_AT = 120

f32 = jnp.float32
bf16 = jnp.bfloat16

HBM = pl.BlockSpec(memory_space=pltpu.HBM)
ANY = pl.BlockSpec(memory_space=pl.ANY)
VMEM = pl.BlockSpec(memory_space=pltpu.VMEM)
SMEM = pl.BlockSpec(memory_space=pltpu.SMEM)
DMA = pltpu.SemaphoreType.DMA


def shape(dims, dtype):
    return jax.ShapeDtypeStruct(dims, dtype)


def call(body, name, flops, size, room=VMEM_BYTES, **kw):
    return pl.pallas_call(
        body,
        name=name,
        compiler_params=pltpu.CompilerParams(vmem_limit_bytes=room),
        cost_estimate=pl.CostEstimate(flops=flops, bytes_accessed=size, transcendentals=0),
        **kw,
    )


def dot(a, b):
    return jnp.dot(a, b, preferred_element_type=f32)


def my_place():
    return lax.axis_index("gz_0") * 4 + lax.axis_index("gz_1")


def send_selected(sel, blocks, out, sems):
    copies = [
        pltpu.make_async_copy(blocks.at[jnp.maximum(sel(q) - 1, 0)], out.at[q], sems.at[q])
        for q in range(GROUP)
    ]
    for c in copies:
        c.start()
    for c in copies:
        c.wait()


def outgoing_kernel(root, block, rows, out, sel, split, root_s, block_s, sem, sems):
    loads = [
        pltpu.make_async_copy(root, root_s, sem.at[0]),
        pltpu.make_async_copy(block, block_s, sem.at[1]),
        pltpu.make_async_copy(rows.at[pl.ds(OWN, SPLIT)], split, sem.at[2]),
    ]
    for c in loads:
        c.start()
    for c in loads:
        c.wait()
    mine = my_place()
    for q in range(GROUP):
        held = jnp.int32(0)
        for j in range(HOST):
            held = jnp.where(root_s[q * HOST + j] == mine, block_s[q * HOST + j] + 1, held)
        sel[q] = held
    send_selected(lambda q: sel[q], split, out, sems)


def tables_kernel(root, cols, present, sel, rows, table, rows_v, sem):
    load_rows = pltpu.make_async_copy(rows, rows_v, sem)
    load_rows.start()
    mine = my_place()

    def slots(b, carry):
        for k in range(K):
            table[b * K + k] = jnp.where(present[b, k] > 0, cols[b, k], SLOTS)
        return carry

    lax.fori_loop(0, SLOTS, slots, 0)
    for h in range(HOST):
        table[ROOTS_AT + h] = root[mine * HOST + h]
    for q in range(GROUP):
        table[SEL_AT + q] = sel[q]
    load_rows.wait()


def tile_copy(tiles, tbuf, tsem, first, i):
    return pltpu.make_async_copy(tiles.at[first + i], tbuf.at[i], tsem.at[i])


def load_tiles(tiles, tbuf, tsem, first, count):
    lax.fori_loop(0, count, lambda i, c: (tile_copy(tiles, tbuf, tsem, first, i).start(), c)[1], 0)


def tile_row(table, tiles, tbuf, tsem, first, i, view):
    tile_copy(tiles, tbuf, tsem, first, i).wait()
    b = first + i
    acc = None
    for k in range(0, K, 2):
        left = jnp.concatenate([tbuf[i, k], tbuf[i, k + 1]], axis=1)
        right = jnp.concatenate([view[table[b * K + k]], view[table[b * K + k + 1]]], axis=0)
        term = dot(left, right)
        acc = term if acc is None else acc + term
    return acc


def replica_rows(table, tiles, out, view, tbuf, obuf, tsem, osem):
    def send(h):
        return pltpu.make_async_copy(obuf.at[h], out.at[table[ROOTS_AT + h]], osem.at[h])

    def step(h, carry):
        obuf[h] = tile_row(table, tiles, tbuf, tsem, ROOTED, h, view).astype(bf16)

        @pl.when(h > 0)
        def _():
            send(h - 1).start()

        return carry

    lax.fori_loop(0, HOST, step, 0)
    send(HOST - 1).start()
    lax.fori_loop(0, HOST, lambda h, c: (send(h).wait(), c)[1], 0)


def replica_kernel(table, rows, incoming, tiles, out, view, tbuf, obuf, tsem, osem):
    load_tiles(tiles, tbuf, tsem, ROOTED, HOST)

    def own(b, carry):
        view[b] = rows[b]
        return carry

    def hosted(h, carry):
        view[ROOTED + h] = incoming[table[ROOTS_AT + h]]
        return carry

    lax.fori_loop(0, ROOTED, own, 0)
    lax.fori_loop(0, HOST, hosted, 0)
    view[SLOTS] = jnp.zeros((TILE, F), bf16)
    replica_rows(table, tiles, out, view, tbuf, obuf, tsem, osem)


def own_kernel(table, view, tiles, w_self, w_neigh, first_own, self_split, part_split, sums, tbuf, tsem):
    load_tiles(tiles, tbuf, tsem, 0, ROOTED)
    sums[...] = jnp.zeros((2, F), f32)

    def own(b, carry):
        neighbours = tile_row(table, tiles, tbuf, tsem, 0, b, view).astype(bf16)
        first = dot(view[b], w_self[...]) + dot(neighbours, w_neigh[...])
        first_own[b] = first
        sums[0:1] += jnp.sum(first, axis=0, keepdims=True)
        sums[1:2] += jnp.sum(first * first, axis=0, keepdims=True)
        return carry

    def split(s, carry):
        part_split[s] = tile_row(table, tiles, tbuf, tsem, 0, OWN + s, view)
        self_split[s] = dot(view[OWN + s], w_self[...])
        return carry

    lax.fori_loop(0, OWN, own, 0)
    lax.fori_loop(0, SPLIT, split, 0)


def add_replicas(table, incoming, total):
    for q in range(GROUP):
        s = table[SEL_AT + q]

        @pl.when(s > 0)
        def _(q=q, s=s):
            total[s - 1] += incoming[q].astype(f32)


def split_kernel(
    table, incoming, part_split, self_split, own_sums, w_neigh, first_split, out, sums, total, pay, sems
):
    total[...] = part_split[...]
    add_replicas(table, incoming, total)
    for s in range(SPLIT):
        first_split[s] = self_split[s] + dot(total[s].astype(bf16), w_neigh[...])
    s1, s2 = own_sums[0:1], own_sums[1:2]
    for s in range(SPLIT):
        first = first_split[s]
        s1 += jnp.sum(first, axis=0, keepdims=True)
        s2 += jnp.sum(first * first, axis=0, keepdims=True)
    sums[0:1] = s1
    sums[1:2] = s2
    center = (s1 * (1.0 / (ROOTED * TILE))).astype(bf16)
    shift = center.astype(f32)
    for s in range(SPLIT):
        pay[s, pl.ds(0, TILE)] = (first_split[s] - shift).astype(bf16)
        pay[s, pl.ds(TILE, CENTER_ROWS)] = jnp.broadcast_to(center, (CENTER_ROWS, F))
    send_selected(lambda q: table[SEL_AT + q], pay, out, sems)


def hidden_kernel(
    count, table, sums, scale, shift, first_own, first_split, incoming, tiles,
    out, view, tbuf, obuf, tsem, osem,
):
    load_tiles(tiles, tbuf, tsem, ROOTED, HOST)
    total = jnp.sum(sums[...], axis=0)
    mean = total[0:1] * (1.0 / count)
    var = total[1:2] * (1.0 / count) - mean * mean
    inv = lax.rsqrt(var + 1e-5)

    def norm(first, less):
        return jax.nn.relu((first - less) * inv * scale[...] + shift[...]).astype(bf16)

    def own(b, carry):
        view[b] = norm(first_own[b], mean)
        return carry

    def split(s, carry):
        view[OWN + s] = norm(first_split[s], mean)
        return carry

    def hosted(h, carry):
        q = table[ROOTS_AT + h]
        centered = incoming[q, pl.ds(0, TILE)].astype(f32)
        center = incoming[q, pl.ds(TILE, CENTER_ROWS)].astype(f32)[0:1]
        view[ROOTED + h] = norm(centered, mean - center)
        return carry

    lax.fori_loop(0, OWN, own, 0)
    lax.fori_loop(0, SPLIT, split, 0)
    lax.fori_loop(0, HOST, hosted, 0)
    view[SLOTS] = jnp.zeros((TILE, F), bf16)
    replica_rows(table, tiles, out, view, tbuf, obuf, tsem, osem)


def own_two_kernel(table, view, tiles, w_self, w_neigh, out, self_split, part_split, tbuf, tsem):
    load_tiles(tiles, tbuf, tsem, 0, ROOTED)

    def own(b, carry):
        neighbours = tile_row(table, tiles, tbuf, tsem, 0, b, view).astype(bf16)
        second = dot(view[b], w_self[...]) + dot(neighbours, w_neigh[...])
        out[b] = second.astype(bf16)
        return carry

    def split(s, carry):
        part_split[s] = tile_row(table, tiles, tbuf, tsem, 0, OWN + s, view)
        self_split[s] = dot(view[OWN + s], w_self[...])
        return carry

    lax.fori_loop(0, OWN, own, 0)
    lax.fori_loop(0, SPLIT, split, 0)


def last_kernel(table, incoming, part_split, self_split, w_neigh, begun, out, total, done, sem):
    total[...] = part_split[...]
    add_replicas(table, incoming, total)
    for s in range(SPLIT):
        done[s] = (self_split[s] + dot(total[s].astype(bf16), w_neigh[...])).astype(bf16)
    put = pltpu.make_async_copy(done, out.at[pl.ds(OWN, SPLIT)], sem)
    put.start()
    put.wait()


MAC = 2 * TILE * TILE * F


def per_device(
    features, tile_values, tile_columns, tile_present, host_root, host_block,
    self_one, neigh_one, scale_one, shift_one, self_two, neigh_two,
):
    rows = features.reshape(ROOTED, TILE, F)
    scale, shift = scale_one.reshape(1, F), shift_one.reshape(1, F)
    count = features.shape[0] * lax.axis_size(GX_GY_GZ)
    wire = pltpu.HBM((GROUP, TILE, F), bf16)
    split_f32 = pltpu.VMEM((SPLIT, TILE, F), f32)
    view_v = pltpu.VMEM((SLOTS + 1, TILE, F), bf16)
    row_buffer = pltpu.VMEM((HOST, TILE, F), bf16)

    def tile_rows(n):
        return pltpu.VMEM((n, K, TILE, TILE), bf16)

    def exchange(blocks, axes=GZ):
        return lax.all_to_all(blocks, axes, split_axis=0, concat_axis=0, tiled=True)

    outgoing, sel = call(
        outgoing_kernel, "outgoing", 0, 2 << 20, room=60 << 20,
        out_shape=(wire, shape((GROUP,), jnp.int32)),
        in_specs=[HBM] * 3,
        out_specs=(HBM, SMEM),
        scratch_shapes=[
            pltpu.VMEM((SPLIT, TILE, F), bf16),
            pltpu.SMEM((GROUP * HOST,), jnp.int32),
            pltpu.SMEM((GROUP * HOST,), jnp.int32),
            DMA((3,)), DMA((GROUP,)),
        ],
    )(host_root, host_block, rows)
    incoming = exchange(outgoing)

    table, rows_v = call(
        tables_kernel, "tables", 0, 8 << 20,
        out_shape=(
            shape((SEL_AT + GROUP,), jnp.int32),
            pltpu.VMEM((ROOTED, TILE, F), bf16),
        ),
        in_specs=[SMEM] * 4 + [HBM],
        out_specs=(SMEM, VMEM),
        scratch_shapes=[DMA],
    )(host_root, tile_columns, tile_present, sel, rows)

    outgoing, view = call(
        replica_kernel, "replicas", 64 * MAC, 4 << 20,
        out_shape=(wire, view_v),
        in_specs=[SMEM] + [VMEM] * 2 + [HBM],
        out_specs=(HBM, VMEM),
        scratch_shapes=[tile_rows(HOST), row_buffer, DMA((HOST,)), DMA((HOST,))],
    )(table, rows_v, incoming, tile_values)
    returned = exchange(outgoing)

    first_own, self_split, part_split, own_sums = call(
        own_kernel, "own_rows", 60 * MAC, 5 << 20,
        out_shape=(pltpu.VMEM((OWN, TILE, F), f32), split_f32, split_f32, pltpu.VMEM((2, F), f32)),
        in_specs=[SMEM, VMEM, HBM, VMEM, VMEM],
        out_specs=(VMEM,) * 4,
        scratch_shapes=[tile_rows(ROOTED), DMA((ROOTED,))],
    )(table, view, tile_values, self_one, neigh_one)

    first_split, outgoing, sums = call(
        split_kernel, "split_rows", 4 * MAC, 3 << 20,
        out_shape=(
            split_f32,
            pltpu.HBM((GROUP, TILE + CENTER_ROWS, F), bf16),
            pltpu.VMEM((2, F), f32),
        ),
        in_specs=[SMEM] + [VMEM] * 5,
        out_specs=(VMEM, HBM, VMEM),
        scratch_shapes=[
            pltpu.VMEM((SPLIT, TILE, F), f32),
            pltpu.VMEM((SPLIT, TILE + CENTER_ROWS, F), bf16),
            DMA((GROUP,)),
        ],
    )(table, returned, part_split, self_split, own_sums, neigh_one)
    incoming = exchange(outgoing)
    sums = lax.psum(lax.psum(sums, "gx"), "gy_1")
    incoming, sums = lax.optimization_barrier((incoming, sums))
    sums = exchange(jnp.broadcast_to(sums, (2 * GROUP, 2, F)), REST)

    outgoing, view = call(
        functools.partial(hidden_kernel, count), "hidden_replicas", 64 * MAC, 5 << 20,
        out_shape=(wire, view_v),
        in_specs=[SMEM] + [VMEM] * 6 + [HBM],
        out_specs=(HBM, VMEM),
        scratch_shapes=[tile_rows(HOST), row_buffer, DMA((HOST,)), DMA((HOST,))],
    )(table, sums, scale, shift, first_own, first_split, incoming, tile_values)
    returned = exchange(outgoing)

    begun, self_split, part_split = call(
        own_two_kernel, "own_rows_two", 60 * MAC, 5 << 20,
        out_shape=(shape((ROOTED, TILE, F), bf16), split_f32, split_f32),
        in_specs=[SMEM, VMEM, HBM, VMEM, VMEM],
        out_specs=(VMEM,) * 3,
        scratch_shapes=[tile_rows(ROOTED), DMA((ROOTED,))],
    )(table, view, tile_values, self_two, neigh_two)

    embedding = call(
        last_kernel, "split_rows_two", 4 * MAC, 3 << 20,
        out_shape=shape((ROOTED, TILE, F), bf16),
        in_specs=[SMEM] + [VMEM] * 4 + [ANY],
        out_specs=ANY,
        input_output_aliases={5: 0},
        scratch_shapes=[pltpu.VMEM((SPLIT, TILE, F), f32), pltpu.VMEM((SPLIT, TILE, F), bf16), DMA],
    )(table, returned, part_split, self_split, neigh_two, begun)
    return embedding.reshape(ROOTED * TILE, F)


def solution(mesh):
    finer = Mesh(
        mesh.devices.reshape(mesh.shape["gx"], 2, 2, 4, 4), ("gx", "gy_0", "gy_1", "gz_0", "gz_1")
    )
    return jax.shard_map(
        per_device,
        mesh=finer,
        in_specs=(
            P(GX_GY_GZ, None),
            P(GX_GY_GZ, None, None, None),
            P(GX_GY_GZ, None),
            P(GX_GY_GZ, None),
            P(GX_GY),
            P(GX_GY),
            P(),
            P(),
            P(),
            P(),
            P(),
            P(),
        ),
        out_specs=P(GX_GY_GZ, None),
        check_vma=False,
    )
```

```python
import functools

import jax
import jax.numpy as jnp
from jax import lax
from jax.experimental import pallas as pl
from jax.experimental.pallas import tpu as pltpu
from jax.sharding import Mesh
from jax.sharding import PartitionSpec as P

OWN = 4
SPLIT = 2
ROOTED = 6
HOST = 8
SLOTS = 14
K = 8
TILE = 128
F = 256
GROUP = 16
CENTER_ROWS = 16
VMEM_BYTES = 50 << 20
GZ = ("gz_0", "gz_1")
GX_GY_GZ = ("gx", "gy_0", "gy_1", "gz_0", "gz_1")
GX_GY = ("gx", "gy_0", "gy_1")
COLUMN = ("gy_0", "gy_1", "gz_1")
ROOTS_AT = 112
SEL_AT = 120

f32 = jnp.float32
bf16 = jnp.bfloat16

HBM = pl.BlockSpec(memory_space=pltpu.HBM)
ANY = pl.BlockSpec(memory_space=pl.ANY)
VMEM = pl.BlockSpec(memory_space=pltpu.VMEM)
SMEM = pl.BlockSpec(memory_space=pltpu.SMEM)
DMA = pltpu.SemaphoreType.DMA


def shape(dims, dtype):
    return jax.ShapeDtypeStruct(dims, dtype)


def call(body, name, flops, size, room=VMEM_BYTES, **kw):
    return pl.pallas_call(
        body,
        name=name,
        compiler_params=pltpu.CompilerParams(vmem_limit_bytes=room),
        cost_estimate=pl.CostEstimate(flops=flops, bytes_accessed=size, transcendentals=0),
        **kw,
    )


def dot(a, b):
    return jnp.dot(a, b, preferred_element_type=f32)


def my_place():
    return lax.axis_index("gz_0") * 4 + lax.axis_index("gz_1")


def loop(n, step):
    lax.fori_loop(0, n, lambda i, c: (step(i), c)[1], 0)


def outgoing_kernel(root, block, rows, out, sel, split, root_s, block_s, sem, sems):
    loads = [
        pltpu.make_async_copy(root, root_s, sem.at[0]),
        pltpu.make_async_copy(block, block_s, sem.at[1]),
        pltpu.make_async_copy(rows.at[pl.ds(OWN, SPLIT)], split, sem.at[2]),
    ]
    for c in loads:
        c.start()
    for c in loads:
        c.wait()
    mine = my_place()

    def send(q, chosen):
        return pltpu.make_async_copy(split.at[chosen], out.at[q], sems.at[q])

    def select(q):
        held = jnp.int32(0)
        for j in range(HOST):
            held = jnp.where(root_s[q * HOST + j] == mine, block_s[q * HOST + j] + 1, held)
        sel[q] = held
        send(q, jnp.maximum(held - 1, 0)).start()

    loop(GROUP, select)
    loop(GROUP, lambda q: send(q, 0).wait())


def tables_kernel(root, cols, present, sel, rows, table, view, sem):
    load_rows = pltpu.make_async_copy(rows, view.at[pl.ds(0, ROOTED)], sem)
    load_rows.start()
    mine = my_place()

    def slots(b):
        for k in range(K):
            table[b * K + k] = jnp.where(present[b, k] > 0, cols[b, k], SLOTS)

    loop(SLOTS, slots)
    for h in range(HOST):
        table[ROOTS_AT + h] = root[mine * HOST + h]
    for q in range(GROUP):
        table[SEL_AT + q] = sel[q]
    view[SLOTS] = jnp.zeros((TILE, F), bf16)
    load_rows.wait()


def tile_copy(tiles, tbuf, tsem, first, i):
    return pltpu.make_async_copy(tiles.at[first + i], tbuf.at[i], tsem.at[i])


def load_tiles(tiles, tbuf, tsem, first, count):
    loop(count, lambda i: tile_copy(tiles, tbuf, tsem, first, i).start())


def tile_row(table, tiles, tbuf, tsem, first, i, view):
    tile_copy(tiles, tbuf, tsem, first, i).wait()
    b = first + i
    acc = None
    for k in range(0, K, 2):
        left = jnp.concatenate([tbuf[i, k], tbuf[i, k + 1]], axis=1)
        right = jnp.concatenate([view[table[b * K + k]], view[table[b * K + k + 1]]], axis=0)
        term = dot(left, right)
        acc = term if acc is None else acc + term
    return acc


def replica_rows(table, tiles, out, view, tbuf, obuf, tsem, osem):
    def send(h):
        return pltpu.make_async_copy(obuf.at[h], out.at[table[ROOTS_AT + h]], osem.at[h])

    def step(h):
        obuf[h] = tile_row(table, tiles, tbuf, tsem, ROOTED, h, view).astype(bf16)

        @pl.when(h > 0)
        def _():
            send(h - 1).start()

    loop(HOST, step)
    send(HOST - 1).start()
    loop(HOST, lambda h: send(h).wait())


def replica_kernel(table, begun, incoming, tiles, out, view, tbuf, obuf, vsem, tsem, osem):
    def hosted(h):
        return pltpu.make_async_copy(
            incoming.at[table[ROOTS_AT + h]], view.at[ROOTED + h], vsem.at[h]
        )

    loop(HOST, lambda h: hosted(h).start())
    load_tiles(tiles, tbuf, tsem, ROOTED, HOST)
    loop(HOST, lambda h: hosted(h).wait())
    replica_rows(table, tiles, out, view, tbuf, obuf, tsem, osem)


def own_kernel(table, view, tiles, w_self, w_neigh, first_own, self_split, part_split, sums, tbuf, tsem):
    load_tiles(tiles, tbuf, tsem, 0, ROOTED)
    sums[...] = jnp.zeros((2, F), f32)

    def own(b, carry):
        neighbours = tile_row(table, tiles, tbuf, tsem, 0, b, view).astype(bf16)
        first = dot(view[b], w_self[...]) + dot(neighbours, w_neigh[...])
        first_own[b] = first
        sums[0:1] += jnp.sum(first, axis=0, keepdims=True)
        sums[1:2] += jnp.sum(first * first, axis=0, keepdims=True)
        return carry

    def split(s, carry):
        part_split[s] = tile_row(table, tiles, tbuf, tsem, 0, OWN + s, view)
        self_split[s] = dot(view[OWN + s], w_self[...])
        return carry

    lax.fori_loop(0, OWN, own, 0)
    lax.fori_loop(0, SPLIT, split, 0)


def add_replicas(table, incoming, total):
    def add(q):
        s = table[SEL_AT + q]

        @pl.when(s > 0)
        def _():
            total[s - 1] += incoming[q].astype(f32)

    loop(GROUP, add)


def split_kernel(table, incoming, part_split, self_split, own_sums, w_neigh, first_split, sums, total):
    total[...] = part_split[...]
    add_replicas(table, incoming, total)
    s1, s2 = own_sums[0:1], own_sums[1:2]
    for s in range(SPLIT):
        first = self_split[s] + dot(total[s].astype(bf16), w_neigh[...])
        first_split[s] = first
        s1 += jnp.sum(first, axis=0, keepdims=True)
        s2 += jnp.sum(first * first, axis=0, keepdims=True)

    def fill(q):
        sums[q, 0:1] = s1
        sums[q, 1:2] = s2

    loop(GROUP, fill)


def centered_kernel(table, first_split, sums, out, pay, sems):
    center = (sums[0, 0:1] * (1.0 / (ROOTED * TILE))).astype(bf16)
    shift = center.astype(f32)

    def fill(s):
        pay[s, pl.ds(0, TILE)] = (first_split[s] - shift).astype(bf16)
        pay[s, pl.ds(TILE, CENTER_ROWS)] = jnp.broadcast_to(center, (CENTER_ROWS, F))

    def send(q):
        chosen = jnp.maximum(table[SEL_AT + q] - 1, 0)
        return pltpu.make_async_copy(pay.at[chosen], out.at[q], sems.at[q])

    loop(SPLIT, fill)
    loop(GROUP, lambda q: send(q).start())
    loop(GROUP, lambda q: send(q).wait())


def hidden_kernel(
    count, table, sums, scale, shift, first_own, first_split, incoming, tiles,
    out, view, tbuf, obuf, tsem, osem,
):
    load_tiles(tiles, tbuf, tsem, ROOTED, HOST)
    mean = sums[0:1] * (1.0 / count)
    var = sums[1:2] * (1.0 / count) - mean * mean
    inv = lax.rsqrt(var + 1e-5)

    def norm(first, less):
        return jax.nn.relu((first - less) * inv * scale[...] + shift[...]).astype(bf16)

    def own(b, carry):
        view[b] = norm(first_own[b], mean)
        return carry

    def split(s, carry):
        view[OWN + s] = norm(first_split[s], mean)
        return carry

    def hosted(h, carry):
        q = table[ROOTS_AT + h]
        centered = incoming[q, pl.ds(0, TILE)].astype(f32)
        center = incoming[q, pl.ds(TILE, CENTER_ROWS)].astype(f32)[0:1]
        view[ROOTED + h] = norm(centered, mean - center)
        return carry

    lax.fori_loop(0, OWN, own, 0)
    lax.fori_loop(0, SPLIT, split, 0)
    lax.fori_loop(0, HOST, hosted, 0)
    view[SLOTS] = jnp.zeros((TILE, F), bf16)
    replica_rows(table, tiles, out, view, tbuf, obuf, tsem, osem)


def own_two_kernel(table, view, tiles, w_self, w_neigh, out, self_split, part_split, tbuf, tsem):
    load_tiles(tiles, tbuf, tsem, 0, ROOTED)

    def own(b, carry):
        neighbours = tile_row(table, tiles, tbuf, tsem, 0, b, view).astype(bf16)
        second = dot(view[b], w_self[...]) + dot(neighbours, w_neigh[...])
        out[b] = second.astype(bf16)
        return carry

    def split(s, carry):
        part_split[s] = tile_row(table, tiles, tbuf, tsem, 0, OWN + s, view)
        self_split[s] = dot(view[OWN + s], w_self[...])
        return carry

    lax.fori_loop(0, OWN, own, 0)
    lax.fori_loop(0, SPLIT, split, 0)


def last_kernel(table, incoming, part_split, self_split, w_neigh, begun, out, total, done, sem):
    total[...] = part_split[...]
    add_replicas(table, incoming, total)
    for s in range(SPLIT):
        done[s] = (self_split[s] + dot(total[s].astype(bf16), w_neigh[...])).astype(bf16)
    put = pltpu.make_async_copy(done, out.at[pl.ds(OWN, SPLIT)], sem)
    put.start()
    put.wait()


MAC = 2 * TILE * TILE * F


def per_device(
    features, tile_values, tile_columns, tile_present, host_root, host_block,
    self_one, neigh_one, scale_one, shift_one, self_two, neigh_two,
):
    rows = features.reshape(ROOTED, TILE, F)
    scale, shift = scale_one.reshape(1, F), shift_one.reshape(1, F)
    count = features.shape[0] * lax.axis_size(GX_GY_GZ)
    wire = pltpu.HBM((GROUP, TILE, F), bf16)
    split_f32 = pltpu.VMEM((SPLIT, TILE, F), f32)
    view_v = pltpu.VMEM((SLOTS + 1, TILE, F), bf16)
    row_buffer = pltpu.VMEM((HOST, TILE, F), bf16)

    def tile_rows(n):
        return pltpu.VMEM((n, K, TILE, TILE), bf16)

    def exchange(blocks, axes=GZ):
        return lax.all_to_all(blocks, axes, split_axis=0, concat_axis=0, tiled=True)

    outgoing, sel = call(
        outgoing_kernel, "outgoing", 0, 2 << 20, room=60 << 20,
        out_shape=(wire, pltpu.SMEM((GROUP,), jnp.int32)),
        in_specs=[HBM] * 3,
        out_specs=(HBM, SMEM),
        scratch_shapes=[
            pltpu.VMEM((SPLIT, TILE, F), bf16),
            pltpu.SMEM((GROUP * HOST,), jnp.int32),
            pltpu.SMEM((GROUP * HOST,), jnp.int32),
            DMA((3,)), DMA((GROUP,)),
        ],
    )(host_root, host_block, rows)
    incoming = exchange(outgoing)

    table, view = call(
        tables_kernel, "tables", 0, 8 << 20,
        out_shape=(
            pltpu.SMEM((SEL_AT + GROUP,), jnp.int32),
            view_v,
        ),
        in_specs=[SMEM] * 4 + [HBM],
        out_specs=(SMEM, VMEM),
        scratch_shapes=[DMA],
    )(host_root, tile_columns, tile_present, sel, rows)

    outgoing, view = call(
        replica_kernel, "replicas", 64 * MAC, 4 << 20,
        out_shape=(wire, view_v),
        in_specs=[SMEM] + [VMEM] * 2 + [HBM],
        out_specs=(HBM, VMEM),
        input_output_aliases={1: 1},
        scratch_shapes=[tile_rows(HOST), row_buffer] + [DMA((HOST,))] * 3,
    )(table, view, incoming, tile_values)
    returned = exchange(outgoing)

    first_own, self_split, part_split, own_sums = call(
        own_kernel, "own_rows", 60 * MAC, 5 << 20,
        out_shape=(pltpu.VMEM((OWN, TILE, F), f32), split_f32, split_f32, pltpu.VMEM((2, F), f32)),
        in_specs=[SMEM, VMEM, HBM, VMEM, VMEM],
        out_specs=(VMEM,) * 4,
        scratch_shapes=[tile_rows(ROOTED), DMA((ROOTED,))],
    )(table, view, tile_values, self_one, neigh_one)

    first_split, sums = call(
        split_kernel, "split_rows", 4 * MAC, 3 << 20,
        out_shape=(split_f32, pltpu.VMEM((GROUP, 2, F), f32)),
        in_specs=[SMEM] + [VMEM] * 5,
        out_specs=(VMEM, VMEM),
        scratch_shapes=[pltpu.VMEM((SPLIT, TILE, F), f32)],
    )(table, returned, part_split, self_split, own_sums, neigh_one)
    column_sums = exchange(sums, COLUMN)
    outgoing = call(
        centered_kernel, "centered", 0, 2 << 20,
        out_shape=pltpu.HBM((GROUP, TILE + CENTER_ROWS, F), bf16),
        in_specs=[SMEM] + [VMEM] * 2,
        out_specs=HBM,
        scratch_shapes=[pltpu.VMEM((SPLIT, TILE + CENTER_ROWS, F), bf16), DMA((GROUP,))],
    )(table, first_split, sums)
    outgoing, column_sums = lax.optimization_barrier((outgoing, column_sums))
    incoming = exchange(outgoing)
    sums = lax.psum(lax.psum(jnp.sum(column_sums, axis=0), "gx"), "gz_0")

    outgoing, view = call(
        functools.partial(hidden_kernel, count), "hidden_replicas", 64 * MAC, 5 << 20,
        out_shape=(wire, view_v),
        in_specs=[SMEM] + [VMEM] * 6 + [HBM],
        out_specs=(HBM, VMEM),
        scratch_shapes=[tile_rows(HOST), row_buffer, DMA((HOST,)), DMA((HOST,))],
    )(table, sums, scale, shift, first_own, first_split, incoming, tile_values)
    returned = exchange(outgoing)

    begun, self_split, part_split = call(
        own_two_kernel, "own_rows_two", 60 * MAC, 5 << 20,
        out_shape=(shape((ROOTED, TILE, F), bf16), split_f32, split_f32),
        in_specs=[SMEM, VMEM, HBM, VMEM, VMEM],
        out_specs=(VMEM,) * 3,
        scratch_shapes=[tile_rows(ROOTED), DMA((ROOTED,))],
    )(table, view, tile_values, self_two, neigh_two)

    embedding = call(
        last_kernel, "split_rows_two", 4 * MAC, 3 << 20,
        out_shape=shape((ROOTED, TILE, F), bf16),
        in_specs=[SMEM] + [VMEM] * 4 + [ANY],
        out_specs=ANY,
        input_output_aliases={5: 0},
        scratch_shapes=[pltpu.VMEM((SPLIT, TILE, F), f32), pltpu.VMEM((SPLIT, TILE, F), bf16), DMA],
    )(table, returned, part_split, self_split, neigh_two, begun)
    return embedding.reshape(ROOTED * TILE, F)


def solution(mesh):
    finer = Mesh(
        mesh.devices.reshape(mesh.shape["gx"], 2, 2, 4, 4), ("gx", "gy_0", "gy_1", "gz_0", "gz_1")
    )
    return jax.shard_map(
        per_device,
        mesh=finer,
        in_specs=(
            P(GX_GY_GZ, None),
            P(GX_GY_GZ, None, None, None),
            P(GX_GY_GZ, None),
            P(GX_GY_GZ, None),
            P(GX_GY),
            P(GX_GY),
            P(),
            P(),
            P(),
            P(),
            P(),
            P(),
        ),
        out_specs=P(GX_GY_GZ, None),
        check_vma=False,
    )
```

```python
import functools

import jax
import jax.numpy as jnp
from jax import lax
from jax.experimental import pallas as pl
from jax.experimental.pallas import tpu as pltpu
from jax.sharding import Mesh
from jax.sharding import PartitionSpec as P

OWN = 4
SPLIT = 2
ROOTED = 6
HOST = 8
SLOTS = 14
K = 8
TILE = 128
CENTER_ROWS = 16
F = 256
GROUP = 16
VMEM_BYTES = 50 << 20
GZ = ("gz_0", "gz_1")
GX_GY_GZ = ("gx", "gy_0", "gy_1", "gz_0", "gz_1")
GX_GY = ("gx", "gy_0", "gy_1")
COLUMN = ("gy_0", "gy_1", "gz_1")
PLANE = ("gx", "gz_0")
PLANE_SIZE = 32
PART = TILE + CENTER_ROWS
ROOTS_AT = 112
SEL_AT = 120
SOURCE_AT = 136
WITHIN_AT = 144
PASS_AT = 152
ENTRIES = 164
SIDE = 4

f32 = jnp.float32
bf16 = jnp.bfloat16

HBM = pl.BlockSpec(memory_space=pltpu.HBM)
ANY = pl.BlockSpec(memory_space=pl.ANY)
VMEM = pl.BlockSpec(memory_space=pltpu.VMEM)
SMEM = pl.BlockSpec(memory_space=pltpu.SMEM)
DMA = pltpu.SemaphoreType.DMA


def shape(dims, dtype):
    return jax.ShapeDtypeStruct(dims, dtype)


def call(body, flops, size, room=VMEM_BYTES, **kw):
    return pl.pallas_call(
        body,
        compiler_params=pltpu.CompilerParams(vmem_limit_bytes=room),
        cost_estimate=pl.CostEstimate(flops=flops, bytes_accessed=size, transcendentals=0),
        **kw,
    )


def dot(a, b):
    return jnp.dot(a, b, preferred_element_type=f32)


def my_place():
    return lax.axis_index("gz_0") * 4 + lax.axis_index("gz_1")


def loop(n, step):
    lax.fori_loop(0, n, lambda i, c: (step(i), c)[1], 0)


def outgoing_kernel(root, block, rows, out, sel, split, root_s, block_s, sem, sems):
    loads = [
        pltpu.make_async_copy(root, root_s, sem.at[0]),
        pltpu.make_async_copy(block, block_s, sem.at[1]),
        pltpu.make_async_copy(rows.at[pl.ds(OWN, SPLIT)], split, sem.at[2]),
    ]
    for c in loads:
        c.start()
    for c in loads:
        c.wait()
    mine = my_place()

    def send(q, chosen):
        return pltpu.make_async_copy(split.at[chosen], out.at[q], sems.at[q])

    def select(q):
        held = jnp.int32(0)
        for j in range(HOST):
            held = jnp.where(root_s[q * HOST + j] == mine, block_s[q * HOST + j] + 1, held)
        sel[q] = held
        send(q, jnp.maximum(held - 1, 0)).start()

    loop(GROUP, select)
    loop(GROUP, lambda q: send(q, 0).wait())


def tables_kernel(root, block, cols, present, sel, rows, table, view, sem):
    load_rows = pltpu.make_async_copy(rows, view.at[pl.ds(0, ROOTED)], sem)
    load_rows.start()
    mine = my_place()
    my_x, my_z = lax.axis_index("gz_0"), lax.axis_index("gz_1")

    def slots(b):
        for k in range(K):
            table[b * K + k] = jnp.where(present[b, k] > 0, cols[b, k], SLOTS)

    def passed_on(i):
        target = ((my_x + 1 + i // SIDE) & (SIDE - 1)) * SIDE + my_z
        source = my_x * SIDE + ((my_z - i) & (SIDE - 1))
        chosen = jnp.int32(0)
        for j in range(HOST):
            at = target * HOST + j
            chosen = jnp.where(root[at] == source, block[at], chosen)
        table[PASS_AT + i] = chosen

    loop(SLOTS, slots)
    loop((SIDE - 1) * SIDE, passed_on)
    for h in range(HOST):
        q = root[mine * HOST + h]
        table[ROOTS_AT + h] = q
        along_x = (my_x - q // SIDE) & (SIDE - 1)
        along_z = (my_z - q) & (SIDE - 1)
        table[SOURCE_AT + h] = jnp.where(along_x == 0, along_z - 1, along_x + SIDE - 2)
        table[WITHIN_AT + h] = jnp.where(along_x == 0, block[mine * HOST + h], along_z)
    for q in range(GROUP):
        table[SEL_AT + q] = sel[q]
    view[SLOTS] = jnp.zeros((TILE, F), bf16)
    load_rows.wait()


def tile_copy(tiles, tbuf, tsem, first, i):
    return pltpu.make_async_copy(tiles.at[first + i], tbuf.at[i], tsem.at[i])


def load_tiles(tiles, tbuf, tsem, first, count):
    loop(count, lambda i: tile_copy(tiles, tbuf, tsem, first, i).start())


def tile_row(table, tiles, tbuf, tsem, first, i, view):
    tile_copy(tiles, tbuf, tsem, first, i).wait()
    b = first + i
    acc = None
    for k in range(0, K, 2):
        left = jnp.concatenate([tbuf[i, k], tbuf[i, k + 1]], axis=1)
        right = jnp.concatenate([view[table[b * K + k]], view[table[b * K + k + 1]]], axis=0)
        term = dot(left, right)
        acc = term if acc is None else acc + term
    return acc


def replica_rows(table, tiles, out, view, tbuf, obuf, tsem, osem):
    def send(h):
        return pltpu.make_async_copy(obuf.at[h], out.at[table[ROOTS_AT + h]], osem.at[h])

    def step(h):
        obuf[h] = tile_row(table, tiles, tbuf, tsem, ROOTED, h, view).astype(bf16)

        @pl.when(h > 0)
        def _():
            send(h - 1).start()

    loop(HOST, step)
    send(HOST - 1).start()
    loop(HOST, lambda h: send(h).wait())


def replica_kernel(table, begun, incoming, tiles, out, view, tbuf, obuf, vsem, tsem, osem):
    def hosted(h):
        return pltpu.make_async_copy(
            incoming.at[table[ROOTS_AT + h]], view.at[ROOTED + h], vsem.at[h]
        )

    loop(HOST, lambda h: hosted(h).start())
    load_tiles(tiles, tbuf, tsem, ROOTED, HOST)
    loop(HOST, lambda h: hosted(h).wait())
    replica_rows(table, tiles, out, view, tbuf, obuf, tsem, osem)


def own_kernel(table, view, tiles, w_self, w_neigh, first_own, self_split, part_split, sums, tbuf, tsem):
    load_tiles(tiles, tbuf, tsem, 0, ROOTED)
    sums[...] = jnp.zeros((2, F), f32)

    def own(b, carry):
        neighbours = tile_row(table, tiles, tbuf, tsem, 0, b, view).astype(bf16)
        first = dot(view[b], w_self[...]) + dot(neighbours, w_neigh[...])
        first_own[b] = first
        sums[0:1] += jnp.sum(first, axis=0, keepdims=True)
        sums[1:2] += jnp.sum(first * first, axis=0, keepdims=True)
        return carry

    def split(s, carry):
        part_split[s] = tile_row(table, tiles, tbuf, tsem, 0, OWN + s, view)
        self_split[s] = dot(view[OWN + s], w_self[...])
        return carry

    lax.fori_loop(0, OWN, own, 0)
    lax.fori_loop(0, SPLIT, split, 0)


def add_replicas(table, incoming, total):
    def add(q):
        s = table[SEL_AT + q]

        @pl.when(s > 0)
        def _():
            total[s - 1] += incoming[q].astype(f32)

    loop(GROUP, add)


def split_kernel(table, incoming, part_split, self_split, own_sums, w_neigh, first_split, sums, parts, total):
    total[...] = part_split[...]
    add_replicas(table, incoming, total)
    s1, s2 = own_sums[0:1], own_sums[1:2]
    for s in range(SPLIT):
        first = self_split[s] + dot(total[s].astype(bf16), w_neigh[...])
        first_split[s] = first
        s1 += jnp.sum(first, axis=0, keepdims=True)
        s2 += jnp.sum(first * first, axis=0, keepdims=True)

    def fill(q):
        sums[q, 0:1] = s1
        sums[q, 1:2] = s2

    loop(GROUP, fill)
    center = (s1 * (1.0 / (ROOTED * TILE))).astype(bf16)
    less = center.astype(f32)
    for s in range(SPLIT):
        parts[s, pl.ds(0, TILE)] = (first_split[s] - less).astype(bf16)
        parts[s, pl.ds(TILE, CENTER_ROWS)] = jnp.broadcast_to(center, (CENTER_ROWS, F))


def again_kernel(column_sums, sums):
    total = jnp.sum(column_sums[...], axis=0)

    def fill(q):
        sums[q] = total

    loop(PLANE_SIZE, fill)


def pass_kernel(table, mine, one, two, three, ahead_one, ahead_two, ahead_three):
    for i, out in enumerate((ahead_one, ahead_two, ahead_three)):
        for j, parts in enumerate((mine, one, two, three)):
            out[j] = parts[table[PASS_AT + i * SIDE + j]]


def hidden_kernel(
    count, table, sums, scale, shift, first_own, first_split, *refs
):
    received, (tiles, out, view, raw, tbuf, obuf, rsem, tsem, osem) = refs[:6], refs[6:]

    def take(h):
        for i, parts in enumerate(received):

            @pl.when(table[SOURCE_AT + h] == i)
            def _():
                pltpu.make_async_copy(
                    parts.at[table[WITHIN_AT + h]], raw.at[h], rsem.at[h]
                ).start()

    loop(HOST, take)
    load_tiles(tiles, tbuf, tsem, ROOTED, HOST)
    total = jnp.sum(sums[...], axis=0)
    mean = total[0:1] * (1.0 / count)
    var = total[1:2] * (1.0 / count) - mean * mean
    inv = lax.rsqrt(var + 1e-5)

    def norm(first, less):
        return jax.nn.relu((first - less) * inv * scale[...] + shift[...]).astype(bf16)

    def own(b):
        view[b] = norm(first_own[b], mean)

    def split(s):
        view[OWN + s] = norm(first_split[s], mean)

    def hosted(h):
        pltpu.make_async_copy(received[0].at[0], raw.at[h], rsem.at[h]).wait()
        centered = raw[h, pl.ds(0, TILE)].astype(f32)
        center = raw[h, pl.ds(TILE, CENTER_ROWS)].astype(f32)[0:1]
        view[ROOTED + h] = norm(centered, mean - center)

    loop(OWN, own)
    loop(SPLIT, split)
    loop(HOST, hosted)
    view[SLOTS] = jnp.zeros((TILE, F), bf16)
    replica_rows(table, tiles, out, view, tbuf, obuf, tsem, osem)


def own_two_kernel(table, view, tiles, w_self, w_neigh, out, self_split, part_split, tbuf, tsem):
    load_tiles(tiles, tbuf, tsem, 0, ROOTED)

    def own(b, carry):
        neighbours = tile_row(table, tiles, tbuf, tsem, 0, b, view).astype(bf16)
        second = dot(view[b], w_self[...]) + dot(neighbours, w_neigh[...])
        out[b] = second.astype(bf16)
        return carry

    def split(s, carry):
        part_split[s] = tile_row(table, tiles, tbuf, tsem, 0, OWN + s, view)
        self_split[s] = dot(view[OWN + s], w_self[...])
        return carry

    lax.fori_loop(0, OWN, own, 0)
    lax.fori_loop(0, SPLIT, split, 0)


def last_kernel(table, incoming, part_split, self_split, w_neigh, begun, out, total, done, sem):
    total[...] = part_split[...]
    add_replicas(table, incoming, total)
    for s in range(SPLIT):
        done[s] = (self_split[s] + dot(total[s].astype(bf16), w_neigh[...])).astype(bf16)
    put = pltpu.make_async_copy(done, out.at[pl.ds(OWN, SPLIT)], sem)
    put.start()
    put.wait()


MAC = 2 * TILE * TILE * F


def layers(
    features, tile_values, tile_columns, tile_present, host_root, host_block,
    self_one, neigh_one, scale_one, shift_one, self_two, neigh_two,
):
    rows = features.reshape(ROOTED, TILE, F)
    scale, shift = scale_one.reshape(1, F), shift_one.reshape(1, F)
    count = features.shape[0] * lax.axis_size(GX_GY_GZ)
    wire = pltpu.HBM((GROUP, TILE, F), bf16)
    split_f32 = pltpu.VMEM((SPLIT, TILE, F), f32)
    view_v = pltpu.VMEM((SLOTS + 1, TILE, F), bf16)
    row_buffer = pltpu.VMEM((HOST, TILE, F), bf16)

    def tile_rows(n):
        return pltpu.VMEM((n, K, TILE, TILE), bf16)

    def exchange(blocks, axes=GZ):
        return lax.all_to_all(blocks, axes, split_axis=0, concat_axis=0, tiled=True)

    outgoing, sel = call(
        outgoing_kernel, 0, 2 << 20, room=60 << 20,
        out_shape=(wire, pltpu.SMEM((GROUP,), jnp.int32)),
        in_specs=[HBM] * 3,
        out_specs=(HBM, SMEM),
        scratch_shapes=[
            pltpu.VMEM((SPLIT, TILE, F), bf16),
            pltpu.SMEM((GROUP * HOST,), jnp.int32),
            pltpu.SMEM((GROUP * HOST,), jnp.int32),
            DMA((3,)), DMA((GROUP,)),
        ],
    )(host_root, host_block, rows)
    incoming = exchange(outgoing)

    table, view = call(
        tables_kernel, 0, 8 << 20,
        out_shape=(
            pltpu.SMEM((ENTRIES,), jnp.int32),
            view_v,
        ),
        in_specs=[SMEM] * 5 + [HBM],
        out_specs=(SMEM, VMEM),
        scratch_shapes=[DMA],
    )(host_root, host_block, tile_columns, tile_present, sel, rows)

    outgoing, view = call(
        replica_kernel, 64 * MAC, 4 << 20,
        out_shape=(wire, view_v),
        in_specs=[SMEM] + [VMEM] * 2 + [HBM],
        out_specs=(HBM, VMEM),
        input_output_aliases={1: 1},
        scratch_shapes=[tile_rows(HOST), row_buffer] + [DMA((HOST,))] * 3,
    )(table, view, incoming, tile_values)
    returned = exchange(outgoing)

    first_own, self_split, part_split, own_sums = call(
        own_kernel, 60 * MAC, 5 << 20,
        out_shape=(pltpu.VMEM((OWN, TILE, F), f32), split_f32, split_f32, pltpu.VMEM((2, F), f32)),
        in_specs=[SMEM, VMEM, HBM, VMEM, VMEM],
        out_specs=(VMEM,) * 4,
        scratch_shapes=[tile_rows(ROOTED), DMA((ROOTED,))],
    )(table, view, tile_values, self_one, neigh_one)

    parts_v = pltpu.VMEM((SPLIT, PART, F), bf16)
    row_v = pltpu.VMEM((SIDE, PART, F), bf16)

    first_split, sums, parts = call(
        split_kernel, 4 * MAC, 3 << 20,
        out_shape=(split_f32, pltpu.VMEM((GROUP, 2, F), f32), parts_v),
        in_specs=[SMEM] + [VMEM] * 5,
        out_specs=(VMEM,) * 3,
        scratch_shapes=[pltpu.VMEM((SPLIT, TILE, F), f32)],
    )(table, returned, part_split, self_split, own_sums, neigh_one)
    sums = exchange(sums, COLUMN)
    column = []
    for d in range(1, SIDE):
        column.append(lax.ppermute(parts, "gz_1", [(i, (i + d) % SIDE) for i in range(SIDE)]))
    sums = call(
        again_kernel, 0, 1 << 17,
        out_shape=pltpu.VMEM((PLANE_SIZE, 2, F), f32),
        in_specs=[VMEM],
        out_specs=VMEM,
    )(sums)
    sums = exchange(sums, PLANE)
    ahead = call(
        pass_kernel, 0, 2 << 20,
        out_shape=(row_v,) * 3,
        in_specs=[SMEM] + [VMEM] * 4,
        out_specs=(VMEM,) * 3,
    )(table, parts, *column)
    row = []
    for d in range(1, SIDE):
        row.append(lax.ppermute(ahead[d - 1], "gz_0", [(i, (i + d) % SIDE) for i in range(SIDE)]))

    outgoing, view = call(
        functools.partial(hidden_kernel, count), 64 * MAC, 5 << 20,
        out_shape=(wire, view_v),
        in_specs=[SMEM] + [VMEM] * 11 + [HBM],
        out_specs=(HBM, VMEM),
        scratch_shapes=[pltpu.VMEM((HOST, PART, F), bf16), tile_rows(HOST), row_buffer]
        + [DMA((HOST,))] * 3,
    )(table, sums, scale, shift, first_own, first_split, *column, *row, tile_values)
    returned = exchange(outgoing)

    begun, self_split, part_split = call(
        own_two_kernel, 60 * MAC, 5 << 20,
        out_shape=(shape((ROOTED, TILE, F), bf16), split_f32, split_f32),
        in_specs=[SMEM, VMEM, HBM, VMEM, VMEM],
        out_specs=(VMEM,) * 3,
        scratch_shapes=[tile_rows(ROOTED), DMA((ROOTED,))],
    )(table, view, tile_values, self_two, neigh_two)

    embedding = call(
        last_kernel, 4 * MAC, 3 << 20,
        out_shape=shape((ROOTED, TILE, F), bf16),
        in_specs=[SMEM] + [VMEM] * 4 + [ANY],
        out_specs=ANY,
        input_output_aliases={5: 0},
        scratch_shapes=[pltpu.VMEM((SPLIT, TILE, F), f32), pltpu.VMEM((SPLIT, TILE, F), bf16), DMA],
    )(table, returned, part_split, self_split, neigh_two, begun)
    return embedding.reshape(ROOTED * TILE, F)


def solution(mesh):
    finer = Mesh(
        mesh.devices.reshape(mesh.shape["gx"], 2, 2, 4, 4), ("gx", "gy_0", "gy_1", "gz_0", "gz_1")
    )
    return jax.shard_map(
        layers,
        mesh=finer,
        in_specs=(
            P(GX_GY_GZ, None),
            P(GX_GY_GZ, None, None, None),
            P(GX_GY_GZ, None),
            P(GX_GY_GZ, None),
            P(GX_GY),
            P(GX_GY),
            P(),
            P(),
            P(),
            P(),
            P(),
            P(),
        ),
        out_specs=P(GX_GY_GZ, None),
        check_vma=False,
    )
```

```python
import functools

import jax
import jax.numpy as jnp
from jax import lax
from jax.experimental import pallas as pl
from jax.experimental.pallas import tpu as pltpu
from jax.sharding import Mesh
from jax.sharding import PartitionSpec as P

OWN = 4
SPLIT = 2
ROOTED = 6
HOST = 8
SLOTS = 14
K = 8
TILE = 128
F = 256
GROUP = 16
CENTER_ROWS = 16
VMEM_BYTES = 50 << 20
GZ = ("gz_0", "gz_1")
GX_GY_GZ = ("gx", "gy_0", "gy_1", "gz_0", "gz_1")
GX_GY = ("gx", "gy_0", "gy_1")
PLANE = ("gx", "gz_0")
PLANE_SIZE = 32
ROOTS_AT = 112
SEL_AT = 120
PASS_AT = 136
ENTRIES = 152
SIDE = 4

f32 = jnp.float32
bf16 = jnp.bfloat16

HBM = pl.BlockSpec(memory_space=pltpu.HBM)
ANY = pl.BlockSpec(memory_space=pl.ANY)
VMEM = pl.BlockSpec(memory_space=pltpu.VMEM)
SMEM = pl.BlockSpec(memory_space=pltpu.SMEM)
DMA = pltpu.SemaphoreType.DMA


def shape(dims, dtype):
    return jax.ShapeDtypeStruct(dims, dtype)


def call(body, flops, size, room=VMEM_BYTES, **kw):
    return pl.pallas_call(
        body,
        compiler_params=pltpu.CompilerParams(vmem_limit_bytes=room),
        cost_estimate=pl.CostEstimate(flops=flops, bytes_accessed=size, transcendentals=0),
        **kw,
    )


def dot(a, b):
    return jnp.dot(a, b, preferred_element_type=f32)


def my_place():
    return lax.axis_index("gz_0") * 4 + lax.axis_index("gz_1")


def loop(n, step):
    lax.fori_loop(0, n, lambda i, c: (step(i), c)[1], 0)


def outgoing_kernel(root, block, rows, out, sel, split, root_s, block_s, sem, sems):
    loads = [
        pltpu.make_async_copy(root, root_s, sem.at[0]),
        pltpu.make_async_copy(block, block_s, sem.at[1]),
        pltpu.make_async_copy(rows.at[pl.ds(OWN, SPLIT)], split, sem.at[2]),
    ]
    for c in loads:
        c.start()
    for c in loads:
        c.wait()
    mine = my_place()

    def send(q, chosen):
        return pltpu.make_async_copy(split.at[chosen], out.at[q], sems.at[q])

    def select(q):
        held = jnp.int32(0)
        for j in range(HOST):
            held = jnp.where(root_s[q * HOST + j] == mine, block_s[q * HOST + j] + 1, held)
        sel[q] = held
        send(q, jnp.maximum(held - 1, 0)).start()

    loop(GROUP, select)
    loop(GROUP, lambda q: send(q, 0).wait())


def tables_kernel(root, block, cols, present, sel, rows, table, view, sem):
    load_rows = pltpu.make_async_copy(rows, view.at[pl.ds(0, ROOTED)], sem)
    load_rows.start()
    mine = my_place()
    my_x, my_z = lax.axis_index("gz_0"), lax.axis_index("gz_1")

    def passed_on(i):
        target, source = (i // SIDE) * SIDE + my_z, my_x * SIDE + (i & (SIDE - 1))
        chosen = jnp.int32(0)
        for j in range(HOST):
            at = target * HOST + j
            chosen = jnp.where(root[at] == source, block[at], chosen)
        table[PASS_AT + i] = chosen

    def slots(b):
        for k in range(K):
            table[b * K + k] = jnp.where(present[b, k] > 0, cols[b, k], SLOTS)

    loop(SLOTS, slots)
    loop(GROUP, passed_on)
    for h in range(HOST):
        table[ROOTS_AT + h] = root[mine * HOST + h]
    for q in range(GROUP):
        table[SEL_AT + q] = sel[q]
    view[SLOTS] = jnp.zeros((TILE, F), bf16)
    load_rows.wait()


def tile_copy(tiles, tbuf, tsem, first, i):
    return pltpu.make_async_copy(tiles.at[first + i], tbuf.at[i], tsem.at[i])


def load_tiles(tiles, tbuf, tsem, first, count):
    loop(count, lambda i: tile_copy(tiles, tbuf, tsem, first, i).start())


def tile_row(table, tiles, tbuf, tsem, first, i, view):
    tile_copy(tiles, tbuf, tsem, first, i).wait()
    b = first + i
    acc = None
    for k in range(0, K, 2):
        left = jnp.concatenate([tbuf[i, k], tbuf[i, k + 1]], axis=1)
        right = jnp.concatenate([view[table[b * K + k]], view[table[b * K + k + 1]]], axis=0)
        term = dot(left, right)
        acc = term if acc is None else acc + term
    return acc


def replica_rows(table, tiles, out, view, tbuf, obuf, tsem, osem):
    def send(h):
        return pltpu.make_async_copy(obuf.at[h], out.at[table[ROOTS_AT + h]], osem.at[h])

    def step(h):
        obuf[h] = tile_row(table, tiles, tbuf, tsem, ROOTED, h, view).astype(bf16)

        @pl.when(h > 0)
        def _():
            send(h - 1).start()

    loop(HOST, step)
    send(HOST - 1).start()
    loop(HOST, lambda h: send(h).wait())


def replica_kernel(table, begun, incoming, tiles, out, view, tbuf, obuf, vsem, tsem, osem):
    def hosted(h):
        return pltpu.make_async_copy(
            incoming.at[table[ROOTS_AT + h]], view.at[ROOTED + h], vsem.at[h]
        )

    loop(HOST, lambda h: hosted(h).start())
    load_tiles(tiles, tbuf, tsem, ROOTED, HOST)
    loop(HOST, lambda h: hosted(h).wait())
    replica_rows(table, tiles, out, view, tbuf, obuf, tsem, osem)


def own_kernel(table, view, tiles, w_self, w_neigh, first_own, self_split, part_split, sums, tbuf, tsem):
    load_tiles(tiles, tbuf, tsem, 0, ROOTED)
    sums[...] = jnp.zeros((2, F), f32)

    def own(b, carry):
        neighbours = tile_row(table, tiles, tbuf, tsem, 0, b, view).astype(bf16)
        first = dot(view[b], w_self[...]) + dot(neighbours, w_neigh[...])
        first_own[b] = first
        sums[0:1] += jnp.sum(first, axis=0, keepdims=True)
        sums[1:2] += jnp.sum(first * first, axis=0, keepdims=True)
        return carry

    def split(s, carry):
        part_split[s] = tile_row(table, tiles, tbuf, tsem, 0, OWN + s, view)
        self_split[s] = dot(view[OWN + s], w_self[...])
        return carry

    lax.fori_loop(0, OWN, own, 0)
    lax.fori_loop(0, SPLIT, split, 0)


def add_replicas(table, incoming, total):
    def add(q):
        s = table[SEL_AT + q]

        @pl.when(s > 0)
        def _():
            total[s - 1] += incoming[q].astype(f32)

    loop(GROUP, add)


def split_kernel(table, incoming, part_split, self_split, own_sums, w_neigh, first_split, sums, parts, total):
    total[...] = part_split[...]
    add_replicas(table, incoming, total)
    s1, s2 = own_sums[0:1], own_sums[1:2]
    for s in range(SPLIT):
        first = self_split[s] + dot(total[s].astype(bf16), w_neigh[...])
        first_split[s] = first
        s1 += jnp.sum(first, axis=0, keepdims=True)
        s2 += jnp.sum(first * first, axis=0, keepdims=True)

    def fill(q):
        sums[q, 0:1] = s1
        sums[q, 1:2] = s2

    loop(PLANE_SIZE, fill)
    center = (s1 * (1.0 / (ROOTED * TILE))).astype(bf16)
    less = center.astype(f32)
    for s in range(SPLIT):
        parts[s, pl.ds(0, TILE)] = (first_split[s] - less).astype(bf16)
        parts[s, pl.ds(TILE, CENTER_ROWS)] = jnp.broadcast_to(center, (CENTER_ROWS, F))


def pass_kernel(table, column, out, sems):
    def send(i):
        chosen = (i & (SIDE - 1)) * SPLIT + table[PASS_AT + i]
        return pltpu.make_async_copy(column.at[chosen], out.at[i], sems.at[i])

    loop(GROUP, lambda i: send(i).start())
    loop(GROUP, lambda i: send(i).wait())


def hidden_kernel(
    count, table, sums, scale, shift, first_own, first_split, incoming, tiles,
    out, view, tbuf, obuf, tsem, osem,
):
    load_tiles(tiles, tbuf, tsem, ROOTED, HOST)
    mean = sums[0:1] * (1.0 / count)
    var = sums[1:2] * (1.0 / count) - mean * mean
    inv = lax.rsqrt(var + 1e-5)

    def norm(first, less):
        return jax.nn.relu((first - less) * inv * scale[...] + shift[...]).astype(bf16)

    def own(b, carry):
        view[b] = norm(first_own[b], mean)
        return carry

    def split(s, carry):
        view[OWN + s] = norm(first_split[s], mean)
        return carry

    def hosted(h, carry):
        q = table[ROOTS_AT + h]
        centered = incoming[q, pl.ds(0, TILE)].astype(f32)
        center = incoming[q, pl.ds(TILE, CENTER_ROWS)].astype(f32)[0:1]
        view[ROOTED + h] = norm(centered, mean - center)
        return carry

    lax.fori_loop(0, OWN, own, 0)
    lax.fori_loop(0, SPLIT, split, 0)
    lax.fori_loop(0, HOST, hosted, 0)
    view[SLOTS] = jnp.zeros((TILE, F), bf16)
    replica_rows(table, tiles, out, view, tbuf, obuf, tsem, osem)


def own_two_kernel(table, view, tiles, w_self, w_neigh, out, self_split, part_split, tbuf, tsem):
    load_tiles(tiles, tbuf, tsem, 0, ROOTED)

    def own(b, carry):
        neighbours = tile_row(table, tiles, tbuf, tsem, 0, b, view).astype(bf16)
        second = dot(view[b], w_self[...]) + dot(neighbours, w_neigh[...])
        out[b] = second.astype(bf16)
        return carry

    def split(s, carry):
        part_split[s] = tile_row(table, tiles, tbuf, tsem, 0, OWN + s, view)
        self_split[s] = dot(view[OWN + s], w_self[...])
        return carry

    lax.fori_loop(0, OWN, own, 0)
    lax.fori_loop(0, SPLIT, split, 0)


def last_kernel(table, incoming, part_split, self_split, w_neigh, begun, out, total, done, sem):
    total[...] = part_split[...]
    add_replicas(table, incoming, total)
    for s in range(SPLIT):
        done[s] = (self_split[s] + dot(total[s].astype(bf16), w_neigh[...])).astype(bf16)
    put = pltpu.make_async_copy(done, out.at[pl.ds(OWN, SPLIT)], sem)
    put.start()
    put.wait()


MAC = 2 * TILE * TILE * F


def layers(
    features, tile_values, tile_columns, tile_present, host_root, host_block,
    self_one, neigh_one, scale_one, shift_one, self_two, neigh_two,
):
    rows = features.reshape(ROOTED, TILE, F)
    scale, shift = scale_one.reshape(1, F), shift_one.reshape(1, F)
    count = features.shape[0] * lax.axis_size(GX_GY_GZ)
    wire = pltpu.HBM((GROUP, TILE, F), bf16)
    split_f32 = pltpu.VMEM((SPLIT, TILE, F), f32)
    view_v = pltpu.VMEM((SLOTS + 1, TILE, F), bf16)
    row_buffer = pltpu.VMEM((HOST, TILE, F), bf16)

    def tile_rows(n):
        return pltpu.VMEM((n, K, TILE, TILE), bf16)

    def exchange(blocks, axes=GZ):
        return lax.all_to_all(blocks, axes, split_axis=0, concat_axis=0, tiled=True)

    outgoing, sel = call(
        outgoing_kernel, 0, 2 << 20, room=60 << 20,
        out_shape=(wire, pltpu.SMEM((GROUP,), jnp.int32)),
        in_specs=[HBM] * 3,
        out_specs=(HBM, SMEM),
        scratch_shapes=[
            pltpu.VMEM((SPLIT, TILE, F), bf16),
            pltpu.SMEM((GROUP * HOST,), jnp.int32),
            pltpu.SMEM((GROUP * HOST,), jnp.int32),
            DMA((3,)), DMA((GROUP,)),
        ],
    )(host_root, host_block, rows)
    incoming = exchange(outgoing)

    table, view = call(
        tables_kernel, 0, 8 << 20,
        out_shape=(
            pltpu.SMEM((ENTRIES,), jnp.int32),
            view_v,
        ),
        in_specs=[SMEM] * 5 + [HBM],
        out_specs=(SMEM, VMEM),
        scratch_shapes=[DMA],
    )(host_root, host_block, tile_columns, tile_present, sel, rows)

    outgoing, view = call(
        replica_kernel, 64 * MAC, 4 << 20,
        out_shape=(wire, view_v),
        in_specs=[SMEM] + [VMEM] * 2 + [HBM],
        out_specs=(HBM, VMEM),
        input_output_aliases={1: 1},
        scratch_shapes=[tile_rows(HOST), row_buffer] + [DMA((HOST,))] * 3,
    )(table, view, incoming, tile_values)
    returned = exchange(outgoing)

    first_own, self_split, part_split, own_sums = call(
        own_kernel, 60 * MAC, 5 << 20,
        out_shape=(pltpu.VMEM((OWN, TILE, F), f32), split_f32, split_f32, pltpu.VMEM((2, F), f32)),
        in_specs=[SMEM, VMEM, HBM, VMEM, VMEM],
        out_specs=(VMEM,) * 4,
        scratch_shapes=[tile_rows(ROOTED), DMA((ROOTED,))],
    )(table, view, tile_values, self_one, neigh_one)

    first_split, sums, parts = call(
        split_kernel, 4 * MAC, 3 << 20,
        out_shape=(
            split_f32,
            pltpu.VMEM((PLANE_SIZE, 2, F), f32),
            pltpu.VMEM((SPLIT, TILE + CENTER_ROWS, F), bf16),
        ),
        in_specs=[SMEM] + [VMEM] * 5,
        out_specs=(VMEM,) * 3,
        scratch_shapes=[pltpu.VMEM((SPLIT, TILE, F), f32)],
    )(table, returned, part_split, self_split, own_sums, neigh_one)
    plane_sums = exchange(sums, PLANE)
    column = lax.all_gather(parts, "gz_1", axis=0, tiled=True)
    column, plane_sums = lax.optimization_barrier((column, plane_sums))
    outgoing = call(
        pass_kernel, 0, 2 << 20,
        out_shape=pltpu.HBM((GROUP, TILE + CENTER_ROWS, F), bf16),
        in_specs=[SMEM, VMEM],
        out_specs=HBM,
        scratch_shapes=[DMA((GROUP,))],
    )(table, column)
    incoming = exchange(outgoing, "gz_0")
    sums = lax.psum(lax.psum(jnp.sum(plane_sums, axis=0), ("gy_0", "gy_1")), "gz_1")

    outgoing, view = call(
        functools.partial(hidden_kernel, count), 64 * MAC, 5 << 20,
        out_shape=(wire, view_v),
        in_specs=[SMEM] + [VMEM] * 6 + [HBM],
        out_specs=(HBM, VMEM),
        scratch_shapes=[tile_rows(HOST), row_buffer, DMA((HOST,)), DMA((HOST,))],
    )(table, sums, scale, shift, first_own, first_split, incoming, tile_values)
    returned = exchange(outgoing)

    begun, self_split, part_split = call(
        own_two_kernel, 60 * MAC, 5 << 20,
        out_shape=(shape((ROOTED, TILE, F), bf16), split_f32, split_f32),
        in_specs=[SMEM, VMEM, HBM, VMEM, VMEM],
        out_specs=(VMEM,) * 3,
        scratch_shapes=[tile_rows(ROOTED), DMA((ROOTED,))],
    )(table, view, tile_values, self_two, neigh_two)

    embedding = call(
        last_kernel, 4 * MAC, 3 << 20,
        out_shape=shape((ROOTED, TILE, F), bf16),
        in_specs=[SMEM] + [VMEM] * 4 + [ANY],
        out_specs=ANY,
        input_output_aliases={5: 0},
        scratch_shapes=[pltpu.VMEM((SPLIT, TILE, F), f32), pltpu.VMEM((SPLIT, TILE, F), bf16), DMA],
    )(table, returned, part_split, self_split, neigh_two, begun)
    return embedding.reshape(ROOTED * TILE, F)


def solution(mesh):
    finer = Mesh(
        mesh.devices.reshape(mesh.shape["gx"], 2, 2, 4, 4), ("gx", "gy_0", "gy_1", "gz_0", "gz_1")
    )
    return jax.shard_map(
        layers,
        mesh=finer,
        in_specs=(
            P(GX_GY_GZ, None),
            P(GX_GY_GZ, None, None, None),
            P(GX_GY_GZ, None),
            P(GX_GY_GZ, None),
            P(GX_GY),
            P(GX_GY),
            P(),
            P(),
            P(),
            P(),
            P(),
            P(),
        ),
        out_specs=P(GX_GY_GZ, None),
        check_vma=False,
    )
```

```python
import functools

import jax
import jax.numpy as jnp
from jax import lax
from jax.experimental import pallas as pl
from jax.experimental.pallas import tpu as pltpu
from jax.sharding import Mesh
from jax.sharding import PartitionSpec as P

OWN = 4
SPLIT = 2
ROOTED = 6
HOST = 8
SLOTS = 14
K = 8
TILE = 128
F = 256
GROUP = 16
CENTER_ROWS = 16
VMEM_BYTES = 50 << 20
GZ = ("gz_0", "gz_1")
GX_GY_GZ = ("gx", "gy_0", "gy_1", "gz_0", "gz_1")
GX_GY = ("gx", "gy_0", "gy_1")
PLANE = ("gx", "gz_0")
PLANE_SIZE = 32
ROOTS_AT = 112
SEL_AT = 120
PASS_AT = 136
ENTRIES = 152
READY = 4
SIDE = 4

f32 = jnp.float32
bf16 = jnp.bfloat16

HBM = pl.BlockSpec(memory_space=pltpu.HBM)
ANY = pl.BlockSpec(memory_space=pl.ANY)
VMEM = pl.BlockSpec(memory_space=pltpu.VMEM)
SMEM = pl.BlockSpec(memory_space=pltpu.SMEM)
DMA = pltpu.SemaphoreType.DMA


def shape(dims, dtype):
    return jax.ShapeDtypeStruct(dims, dtype)


def call(body, flops, size, room=VMEM_BYTES, **kw):
    return pl.pallas_call(
        body,
        compiler_params=pltpu.CompilerParams(vmem_limit_bytes=room),
        cost_estimate=pl.CostEstimate(flops=flops, bytes_accessed=size, transcendentals=0),
        **kw,
    )


def dot(a, b):
    return jnp.dot(a, b, preferred_element_type=f32)


def my_place():
    return lax.axis_index("gz_0") * 4 + lax.axis_index("gz_1")


def loop(n, step):
    lax.fori_loop(0, n, lambda i, c: (step(i), c)[1], 0)


def outgoing_kernel(root, block, rows, out, sel, split, root_s, block_s, sem, sems):
    loads = [
        pltpu.make_async_copy(root, root_s, sem.at[0]),
        pltpu.make_async_copy(block, block_s, sem.at[1]),
        pltpu.make_async_copy(rows.at[pl.ds(OWN, SPLIT)], split, sem.at[2]),
    ]
    for c in loads:
        c.start()
    for c in loads:
        c.wait()
    mine = my_place()

    def send(q, chosen):
        return pltpu.make_async_copy(split.at[chosen], out.at[q], sems)

    def select(q):
        held = jnp.int32(0)
        for j in range(HOST):
            held = jnp.where(root_s[q * HOST + j] == mine, block_s[q * HOST + j] + 1, held)
        sel[q] = held
        send(q, jnp.maximum(held - 1, 0)).start()

    loop(GROUP, select)
    pltpu.make_async_copy(out, out, sems).wait()


def tables_kernel(root, block, cols, present, sel, rows, tiles, table, view, ready, sem):
    load_rows = pltpu.make_async_copy(rows, view.at[pl.ds(0, ROOTED)], sem.at[0])
    load_tiles = pltpu.make_async_copy(tiles.at[pl.ds(ROOTED, READY)], ready, sem.at[1])
    load_rows.start()
    load_tiles.start()
    mine = my_place()
    my_x, my_z = lax.axis_index("gz_0"), lax.axis_index("gz_1")

    def passed_on(i):
        target, source = (i // SIDE) * SIDE + my_z, my_x * SIDE + (i & (SIDE - 1))
        chosen = jnp.int32(0)
        for j in range(HOST):
            at = target * HOST + j
            chosen = jnp.where(root[at] == source, block[at], chosen)
        table[PASS_AT + i] = chosen

    def slots(b):
        for k in range(K):
            table[b * K + k] = jnp.where(present[b, k] > 0, cols[b, k], SLOTS)

    loop(SLOTS, slots)
    loop(GROUP, passed_on)
    for h in range(HOST):
        table[ROOTS_AT + h] = root[mine * HOST + h]
    for q in range(GROUP):
        table[SEL_AT + q] = sel[q]
    view[SLOTS] = jnp.zeros((TILE, F), bf16)
    load_rows.wait()
    load_tiles.wait()


def tile_copy(tiles, tbuf, tsem, first, i):
    return pltpu.make_async_copy(tiles.at[first + i], tbuf.at[i], tsem.at[i])


def load_tiles(tiles, tbuf, tsem, first, count):
    loop(count, lambda i: tile_copy(tiles, tbuf, tsem, first, i).start())


def tile_sum(table, row_tiles, b, view):
    acc = None
    for k in range(0, K, 2):
        left = jnp.concatenate([row_tiles[k], row_tiles[k + 1]], axis=1)
        right = jnp.concatenate([view[table[b * K + k]], view[table[b * K + k + 1]]], axis=0)
        term = dot(left, right)
        acc = term if acc is None else acc + term
    return acc


def tile_row(table, tiles, tbuf, tsem, i, view):
    tile_copy(tiles, tbuf, tsem, 0, i).wait()
    return tile_sum(table, tbuf.at[i], i, view)


def group_copies(tiles, tbuf, tsem, groups):
    return {
        first: pltpu.make_async_copy(
            tiles.at[pl.ds(ROOTED + first, count)], tbuf.at[pl.ds(first, count)], tsem.at[n]
        )
        for n, (first, count) in enumerate(groups)
    }


def replica_rows(table, row_tiles, waits, out, view, obuf, osem):
    def send(h):
        pltpu.make_async_copy(obuf.at[h], out.at[table[ROOTS_AT + h]], osem).start()

    for h in range(HOST):
        if h in waits:
            waits[h].wait()
        obuf[h] = tile_sum(table, row_tiles(h), ROOTED + h, view).astype(bf16)
        if h:
            send(h - 1)
    send(HOST - 1)
    pltpu.make_async_copy(obuf, out.at[pl.ds(0, HOST)], osem).wait()


def replica_kernel(table, begun, incoming, ready, tiles, out, view, tbuf, obuf, vsem, tsem, osem):
    for h in range(HOST):
        pltpu.make_async_copy(
            incoming.at[table[ROOTS_AT + h]], view.at[ROOTED + h], vsem
        ).start()
    later = group_copies(tiles, tbuf, tsem, ((READY, 2), (READY + 2, 2)))
    for c in later.values():
        c.start()
    pltpu.make_async_copy(
        incoming.at[pl.ds(0, HOST)], view.at[pl.ds(ROOTED, HOST)], vsem
    ).wait()
    replica_rows(
        table, lambda h: ready.at[h] if h < READY else tbuf.at[h], later, out, view, obuf, osem
    )


def own_kernel(table, view, tiles, w_self, w_neigh, first_own, self_split, part_split, sums, tbuf, tsem):
    load_tiles(tiles, tbuf, tsem, 0, ROOTED)
    sums[...] = jnp.zeros((2, F), f32)

    def own(b, carry):
        neighbours = tile_row(table, tiles, tbuf, tsem, b, view).astype(bf16)
        first = dot(view[b], w_self[...]) + dot(neighbours, w_neigh[...])
        first_own[b] = first
        sums[0:1] += jnp.sum(first, axis=0, keepdims=True)
        sums[1:2] += jnp.sum(first * first, axis=0, keepdims=True)
        return carry

    def split(s, carry):
        part_split[s] = tile_row(table, tiles, tbuf, tsem, OWN + s, view)
        self_split[s] = dot(view[OWN + s], w_self[...])
        return carry

    lax.fori_loop(0, OWN, own, 0)
    lax.fori_loop(0, SPLIT, split, 0)


def add_replicas(table, incoming, total):
    def add(q):
        s = table[SEL_AT + q]

        @pl.when(s > 0)
        def _():
            total[s - 1] += incoming[q].astype(f32)

    loop(GROUP, add)


def split_kernel(table, incoming, part_split, self_split, own_sums, w_neigh, first_split, sums, parts, total):
    total[...] = part_split[...]
    add_replicas(table, incoming, total)
    s1, s2 = own_sums[0:1], own_sums[1:2]
    for s in range(SPLIT):
        first = self_split[s] + dot(total[s].astype(bf16), w_neigh[...])
        first_split[s] = first
        s1 += jnp.sum(first, axis=0, keepdims=True)
        s2 += jnp.sum(first * first, axis=0, keepdims=True)

    def fill(q):
        sums[q, 0:1] = s1
        sums[q, 1:2] = s2

    loop(PLANE_SIZE, fill)
    center = (s1 * (1.0 / (ROOTED * TILE))).astype(bf16)
    less = center.astype(f32)
    for s in range(SPLIT):
        parts[s, pl.ds(0, TILE)] = (first_split[s] - less).astype(bf16)
        parts[s, pl.ds(TILE, CENTER_ROWS)] = jnp.broadcast_to(center, (CENTER_ROWS, F))


def pass_kernel(table, column, out, sems):
    def send(i):
        chosen = (i & (SIDE - 1)) * SPLIT + table[PASS_AT + i]
        return pltpu.make_async_copy(column.at[chosen], out.at[i], sems)

    loop(GROUP, lambda i: send(i).start())
    pltpu.make_async_copy(out, out, sems).wait()


def hidden_kernel(
    count, table, sums, scale, shift, first_own, first_split, incoming, tiles,
    out, view, tbuf, obuf, tsem, osem,
):
    copies = group_copies(tiles, tbuf, tsem, ((0, 4), (4, 4)))
    for c in copies.values():
        c.start()
    mean = sums[0:1] * (1.0 / count)
    var = sums[1:2] * (1.0 / count) - mean * mean
    inv = lax.rsqrt(var + 1e-5)

    def norm(first, less):
        return jax.nn.relu((first - less) * inv * scale[...] + shift[...]).astype(bf16)

    def own(b, carry):
        view[b] = norm(first_own[b], mean)
        return carry

    def split(s, carry):
        view[OWN + s] = norm(first_split[s], mean)
        return carry

    def hosted(h, carry):
        q = table[ROOTS_AT + h]
        centered = incoming[q, pl.ds(0, TILE)].astype(f32)
        center = incoming[q, pl.ds(TILE, CENTER_ROWS)].astype(f32)[0:1]
        view[ROOTED + h] = norm(centered, mean - center)
        return carry

    lax.fori_loop(0, OWN, own, 0)
    lax.fori_loop(0, SPLIT, split, 0)
    lax.fori_loop(0, HOST, hosted, 0)
    view[SLOTS] = jnp.zeros((TILE, F), bf16)
    replica_rows(table, lambda h: tbuf.at[h], copies, out, view, obuf, osem)


def own_two_kernel(table, view, tiles, w_self, w_neigh, out, self_split, part_split, tbuf, tsem):
    load_tiles(tiles, tbuf, tsem, 0, ROOTED)

    def own(b, carry):
        neighbours = tile_row(table, tiles, tbuf, tsem, b, view).astype(bf16)
        second = dot(view[b], w_self[...]) + dot(neighbours, w_neigh[...])
        out[b] = second.astype(bf16)
        return carry

    def split(s, carry):
        part_split[s] = tile_row(table, tiles, tbuf, tsem, OWN + s, view)
        self_split[s] = dot(view[OWN + s], w_self[...])
        return carry

    lax.fori_loop(0, OWN, own, 0)
    lax.fori_loop(0, SPLIT, split, 0)


def last_kernel(table, incoming, part_split, self_split, w_neigh, begun, out, total, done, sem):
    total[...] = part_split[...]
    add_replicas(table, incoming, total)
    for s in range(SPLIT):
        done[s] = (self_split[s] + dot(total[s].astype(bf16), w_neigh[...])).astype(bf16)
    put = pltpu.make_async_copy(done, out.at[pl.ds(OWN, SPLIT)], sem)
    put.start()
    put.wait()


MAC = 2 * TILE * TILE * F


def layers(
    features, tile_values, tile_columns, tile_present, host_root, host_block,
    self_one, neigh_one, scale_one, shift_one, self_two, neigh_two,
):
    rows = features.reshape(ROOTED, TILE, F)
    scale, shift = scale_one.reshape(1, F), shift_one.reshape(1, F)
    count = features.shape[0] * lax.axis_size(GX_GY_GZ)
    wire = pltpu.HBM((GROUP, TILE, F), bf16)
    split_f32 = pltpu.VMEM((SPLIT, TILE, F), f32)
    view_v = pltpu.VMEM((SLOTS + 1, TILE, F), bf16)
    row_buffer = pltpu.VMEM((HOST, TILE, F), bf16)

    def tile_rows(n):
        return pltpu.VMEM((n, K, TILE, TILE), bf16)

    def exchange(blocks, axes=GZ):
        return lax.all_to_all(blocks, axes, split_axis=0, concat_axis=0, tiled=True)

    outgoing, sel = call(
        outgoing_kernel, 0, 2 << 20, room=60 << 20,
        out_shape=(wire, pltpu.SMEM((GROUP,), jnp.int32)),
        in_specs=[HBM] * 3,
        out_specs=(HBM, SMEM),
        scratch_shapes=[
            pltpu.VMEM((SPLIT, TILE, F), bf16),
            pltpu.SMEM((GROUP * HOST,), jnp.int32),
            pltpu.SMEM((GROUP * HOST,), jnp.int32),
            DMA((3,)), DMA,
        ],
    )(host_root, host_block, rows)
    incoming = exchange(outgoing)

    table, view, ready = call(
        tables_kernel, 0, 8 << 20,
        out_shape=(
            pltpu.SMEM((ENTRIES,), jnp.int32),
            view_v,
            tile_rows(READY),
        ),
        in_specs=[SMEM] * 5 + [HBM] * 2,
        out_specs=(SMEM, VMEM, VMEM),
        scratch_shapes=[DMA((2,))],
    )(host_root, host_block, tile_columns, tile_present, sel, rows, tile_values)

    outgoing, view = call(
        replica_kernel, 64 * MAC, 4 << 20,
        out_shape=(wire, view_v),
        in_specs=[SMEM] + [VMEM] * 3 + [HBM],
        out_specs=(HBM, VMEM),
        input_output_aliases={1: 1},
        scratch_shapes=[tile_rows(HOST), row_buffer, DMA, DMA((2,)), DMA],
    )(table, view, incoming, ready, tile_values)
    returned = exchange(outgoing)

    first_own, self_split, part_split, own_sums = call(
        own_kernel, 60 * MAC, 5 << 20,
        out_shape=(pltpu.VMEM((OWN, TILE, F), f32), split_f32, split_f32, pltpu.VMEM((2, F), f32)),
        in_specs=[SMEM, VMEM, HBM, VMEM, VMEM],
        out_specs=(VMEM,) * 4,
        scratch_shapes=[tile_rows(ROOTED), DMA((ROOTED,))],
    )(table, view, tile_values, self_one, neigh_one)

    first_split, sums, parts = call(
        split_kernel, 4 * MAC, 3 << 20,
        out_shape=(
            split_f32,
            pltpu.VMEM((PLANE_SIZE, 2, F), f32),
            pltpu.VMEM((SPLIT, TILE + CENTER_ROWS, F), bf16),
        ),
        in_specs=[SMEM] + [VMEM] * 5,
        out_specs=(VMEM,) * 3,
        scratch_shapes=[pltpu.VMEM((SPLIT, TILE, F), f32)],
    )(table, returned, part_split, self_split, own_sums, neigh_one)
    plane_sums = exchange(sums, PLANE)
    column = lax.all_gather(parts, "gz_1", axis=0, tiled=True)
    column, plane_sums = lax.optimization_barrier((column, plane_sums))
    outgoing = call(
        pass_kernel, 0, 2 << 20,
        out_shape=pltpu.HBM((GROUP, TILE + CENTER_ROWS, F), bf16),
        in_specs=[SMEM, VMEM],
        out_specs=HBM,
        scratch_shapes=[DMA],
    )(table, column)
    incoming = exchange(outgoing, "gz_0")
    sums = lax.psum(lax.psum(jnp.sum(plane_sums, axis=0), ("gy_0", "gy_1")), "gz_1")

    outgoing, view = call(
        functools.partial(hidden_kernel, count), 64 * MAC, 5 << 20,
        out_shape=(wire, view_v),
        in_specs=[SMEM] + [VMEM] * 6 + [HBM],
        out_specs=(HBM, VMEM),
        scratch_shapes=[tile_rows(HOST), row_buffer, DMA((2,)), DMA],
    )(table, sums, scale, shift, first_own, first_split, incoming, tile_values)
    returned = exchange(outgoing)

    begun, self_split, part_split = call(
        own_two_kernel, 60 * MAC, 5 << 20,
        out_shape=(shape((ROOTED, TILE, F), bf16), split_f32, split_f32),
        in_specs=[SMEM, VMEM, HBM, VMEM, VMEM],
        out_specs=(VMEM,) * 3,
        scratch_shapes=[tile_rows(ROOTED), DMA((ROOTED,))],
    )(table, view, tile_values, self_two, neigh_two)

    embedding = call(
        last_kernel, 4 * MAC, 3 << 20,
        out_shape=shape((ROOTED, TILE, F), bf16),
        in_specs=[SMEM] + [VMEM] * 4 + [ANY],
        out_specs=ANY,
        input_output_aliases={5: 0},
        scratch_shapes=[pltpu.VMEM((SPLIT, TILE, F), f32), pltpu.VMEM((SPLIT, TILE, F), bf16), DMA],
    )(table, returned, part_split, self_split, neigh_two, begun)
    return embedding.reshape(ROOTED * TILE, F)


def solution(mesh):
    finer = Mesh(
        mesh.devices.reshape(mesh.shape["gx"], 2, 2, 4, 4), ("gx", "gy_0", "gy_1", "gz_0", "gz_1")
    )
    return jax.shard_map(
        layers,
        mesh=finer,
        in_specs=(
            P(GX_GY_GZ, None),
            P(GX_GY_GZ, None, None, None),
            P(GX_GY_GZ, None),
            P(GX_GY_GZ, None),
            P(GX_GY),
            P(GX_GY),
            P(),
            P(),
            P(),
            P(),
            P(),
            P(),
        ),
        out_specs=P(GX_GY_GZ, None),
        check_vma=False,
    )
```

```python
import functools

import jax
import jax.numpy as jnp
from jax import lax
from jax.experimental import pallas as pl
from jax.experimental.pallas import tpu as pltpu
from jax.sharding import Mesh
from jax.sharding import PartitionSpec as P

OWN = 4
SPLIT = 2
ROOTED = 6
HOST = 8
SLOTS = 14
K = 8
TILE = 128
F = 256
GROUP = 16
CENTER_ROWS = 16
VMEM_BYTES = 50 << 20
GZ = ("gz_0", "gz_1")
GX_GY_GZ = ("gx", "gy_0", "gy_1", "gz_0", "gz_1")
GX_GY = ("gx", "gy_0", "gy_1")
PLANE = ("gx", "gz_0")
PLANE_SIZE = 32
ROOTS_AT = 112
SEL_AT = 120
ENTRIES = 136
READY = 4
SIDE = 4

f32 = jnp.float32
bf16 = jnp.bfloat16

HBM = pl.BlockSpec(memory_space=pltpu.HBM)
ANY = pl.BlockSpec(memory_space=pl.ANY)
VMEM = pl.BlockSpec(memory_space=pltpu.VMEM)
SMEM = pl.BlockSpec(memory_space=pltpu.SMEM)
DMA = pltpu.SemaphoreType.DMA


def shape(dims, dtype):
    return jax.ShapeDtypeStruct(dims, dtype)


def call(body, flops, size, room=VMEM_BYTES, **kw):
    return pl.pallas_call(
        body,
        compiler_params=pltpu.CompilerParams(vmem_limit_bytes=room),
        cost_estimate=pl.CostEstimate(flops=flops, bytes_accessed=size, transcendentals=0),
        **kw,
    )


def dot(a, b):
    return jnp.dot(a, b, preferred_element_type=f32)


def my_place():
    return lax.axis_index("gz_0") * 4 + lax.axis_index("gz_1")


def loop(n, step):
    lax.fori_loop(0, n, lambda i, c: (step(i), c)[1], 0)


def begin_kernel(root, block, rows, picks, parts, root_s, block_s, sem):
    loads = [
        pltpu.make_async_copy(root, root_s, sem.at[0]),
        pltpu.make_async_copy(block, block_s, sem.at[1]),
        pltpu.make_async_copy(rows.at[pl.ds(OWN, SPLIT)], parts, sem.at[2]),
    ]
    for c in loads:
        c.start()
    for c in loads[:2]:
        c.wait()
    my_x, my_z = lax.axis_index("gz_0"), lax.axis_index("gz_1")

    def pick(i):
        target, source = (i // SIDE) * SIDE + my_z, my_x * SIDE + (i & (SIDE - 1))
        chosen = jnp.int32(0)
        for j in range(HOST):
            at = target * HOST + j
            chosen = jnp.where(root_s[at] == source, block_s[at], chosen)
        picks[i] = chosen

    loop(GROUP, pick)
    loads[2].wait()


def tables_kernel(root, block, cols, present, rows, tiles, table, view, ready, sem):
    load_rows = pltpu.make_async_copy(rows, view.at[pl.ds(0, ROOTED)], sem.at[0])
    load_tiles = pltpu.make_async_copy(tiles.at[pl.ds(ROOTED, READY)], ready, sem.at[1])
    load_rows.start()
    load_tiles.start()
    mine = my_place()

    def select(q):
        held = jnp.int32(0)
        for j in range(HOST):
            held = jnp.where(root[q * HOST + j] == mine, block[q * HOST + j] + 1, held)
        table[SEL_AT + q] = held

    def slots(b):
        for k in range(K):
            table[b * K + k] = jnp.where(present[b, k] > 0, cols[b, k], SLOTS)

    loop(SLOTS, slots)
    loop(GROUP, select)
    for h in range(HOST):
        table[ROOTS_AT + h] = root[mine * HOST + h]
    view[SLOTS] = jnp.zeros((TILE, F), bf16)
    load_rows.wait()
    load_tiles.wait()


def tile_copy(tiles, tbuf, tsem, first, i):
    return pltpu.make_async_copy(tiles.at[first + i], tbuf.at[i], tsem.at[i])


def load_tiles(tiles, tbuf, tsem, first, count):
    loop(count, lambda i: tile_copy(tiles, tbuf, tsem, first, i).start())


def tile_sum(table, row_tiles, b, view):
    acc = None
    for k in range(0, K, 2):
        left = jnp.concatenate([row_tiles[k], row_tiles[k + 1]], axis=1)
        right = jnp.concatenate([view[table[b * K + k]], view[table[b * K + k + 1]]], axis=0)
        term = dot(left, right)
        acc = term if acc is None else acc + term
    return acc


def tile_row(table, tiles, tbuf, tsem, i, view):
    tile_copy(tiles, tbuf, tsem, 0, i).wait()
    return tile_sum(table, tbuf.at[i], i, view)


def group_copies(tiles, tbuf, tsem, groups):
    return {
        first: pltpu.make_async_copy(
            tiles.at[pl.ds(ROOTED + first, count)], tbuf.at[pl.ds(first, count)], tsem.at[n]
        )
        for n, (first, count) in enumerate(groups)
    }


def replica_rows(table, row_tiles, waits, out, view, obuf, osem):
    def send(h):
        pltpu.make_async_copy(obuf.at[h], out.at[table[ROOTS_AT + h]], osem).start()

    for h in range(HOST):
        if h in waits:
            waits[h].wait()
        obuf[h] = tile_sum(table, row_tiles(h), ROOTED + h, view).astype(bf16)
        if h:
            send(h - 1)
    send(HOST - 1)
    pltpu.make_async_copy(obuf, out.at[pl.ds(0, HOST)], osem).wait()


def replica_kernel(table, begun, incoming, ready, tiles, out, view, tbuf, obuf, vsem, tsem, osem):
    for h in range(HOST):
        pltpu.make_async_copy(
            incoming.at[table[ROOTS_AT + h]], view.at[ROOTED + h], vsem
        ).start()
    later = group_copies(tiles, tbuf, tsem, ((READY, 2), (READY + 2, 2)))
    for c in later.values():
        c.start()
    pltpu.make_async_copy(
        incoming.at[pl.ds(0, HOST)], view.at[pl.ds(ROOTED, HOST)], vsem
    ).wait()
    replica_rows(
        table, lambda h: ready.at[h] if h < READY else tbuf.at[h], later, out, view, obuf, osem
    )


def own_kernel(table, view, tiles, w_self, w_neigh, first_own, self_split, part_split, sums, tbuf, tsem):
    load_tiles(tiles, tbuf, tsem, 0, ROOTED)
    sums[...] = jnp.zeros((2, F), f32)

    def own(b, carry):
        neighbours = tile_row(table, tiles, tbuf, tsem, b, view).astype(bf16)
        first = dot(view[b], w_self[...]) + dot(neighbours, w_neigh[...])
        first_own[b] = first
        sums[0:1] += jnp.sum(first, axis=0, keepdims=True)
        sums[1:2] += jnp.sum(first * first, axis=0, keepdims=True)
        return carry

    def split(s, carry):
        part_split[s] = tile_row(table, tiles, tbuf, tsem, OWN + s, view)
        self_split[s] = dot(view[OWN + s], w_self[...])
        return carry

    lax.fori_loop(0, OWN, own, 0)
    lax.fori_loop(0, SPLIT, split, 0)


def add_replicas(table, incoming, total):
    def add(q):
        s = table[SEL_AT + q]

        @pl.when(s > 0)
        def _():
            total[s - 1] += incoming[q].astype(f32)

    loop(GROUP, add)


def split_kernel(table, incoming, part_split, self_split, own_sums, w_neigh, first_split, sums, parts, total):
    total[...] = part_split[...]
    add_replicas(table, incoming, total)
    s1, s2 = own_sums[0:1], own_sums[1:2]
    for s in range(SPLIT):
        first = self_split[s] + dot(total[s].astype(bf16), w_neigh[...])
        first_split[s] = first
        s1 += jnp.sum(first, axis=0, keepdims=True)
        s2 += jnp.sum(first * first, axis=0, keepdims=True)

    def fill(q):
        sums[q, 0:1] = s1
        sums[q, 1:2] = s2

    loop(PLANE_SIZE, fill)
    center = (s1 * (1.0 / (ROOTED * TILE))).astype(bf16)
    less = center.astype(f32)
    for s in range(SPLIT):
        parts[s, pl.ds(0, TILE)] = (first_split[s] - less).astype(bf16)
        parts[s, pl.ds(TILE, CENTER_ROWS)] = jnp.broadcast_to(center, (CENTER_ROWS, F))


def pass_kernel(picks, column, out, sem):
    def send(i):
        chosen = (i & (SIDE - 1)) * SPLIT + picks[i]
        return pltpu.make_async_copy(column.at[chosen], out.at[i], sem)

    loop(GROUP, lambda i: send(i).start())
    pltpu.make_async_copy(out, out, sem).wait()


def hidden_kernel(
    count, table, sums, scale, shift, first_own, first_split, incoming, tiles,
    out, view, tbuf, obuf, tsem, osem,
):
    copies = group_copies(tiles, tbuf, tsem, ((0, 4), (4, 4)))
    for c in copies.values():
        c.start()
    mean = sums[0:1] * (1.0 / count)
    var = sums[1:2] * (1.0 / count) - mean * mean
    inv = lax.rsqrt(var + 1e-5)

    def norm(first, less):
        return jax.nn.relu((first - less) * inv * scale[...] + shift[...]).astype(bf16)

    def own(b, carry):
        view[b] = norm(first_own[b], mean)
        return carry

    def split(s, carry):
        view[OWN + s] = norm(first_split[s], mean)
        return carry

    def hosted(h, carry):
        q = table[ROOTS_AT + h]
        centered = incoming[q, pl.ds(0, TILE)].astype(f32)
        center = incoming[q, pl.ds(TILE, CENTER_ROWS)].astype(f32)[0:1]
        view[ROOTED + h] = norm(centered, mean - center)
        return carry

    lax.fori_loop(0, OWN, own, 0)
    lax.fori_loop(0, SPLIT, split, 0)
    lax.fori_loop(0, HOST, hosted, 0)
    view[SLOTS] = jnp.zeros((TILE, F), bf16)
    replica_rows(table, lambda h: tbuf.at[h], copies, out, view, obuf, osem)


def own_two_kernel(table, view, tiles, w_self, w_neigh, out, self_split, part_split, tbuf, tsem):
    load_tiles(tiles, tbuf, tsem, 0, ROOTED)

    def own(b, carry):
        neighbours = tile_row(table, tiles, tbuf, tsem, b, view).astype(bf16)
        second = dot(view[b], w_self[...]) + dot(neighbours, w_neigh[...])
        out[b] = second.astype(bf16)
        return carry

    def split(s, carry):
        part_split[s] = tile_row(table, tiles, tbuf, tsem, OWN + s, view)
        self_split[s] = dot(view[OWN + s], w_self[...])
        return carry

    lax.fori_loop(0, OWN, own, 0)
    lax.fori_loop(0, SPLIT, split, 0)


def last_kernel(table, incoming, part_split, self_split, w_neigh, begun, out, total, done, sem):
    total[...] = part_split[...]
    add_replicas(table, incoming, total)
    for s in range(SPLIT):
        done[s] = (self_split[s] + dot(total[s].astype(bf16), w_neigh[...])).astype(bf16)
    put = pltpu.make_async_copy(done, out.at[pl.ds(OWN, SPLIT)], sem)
    put.start()
    put.wait()


MAC = 2 * TILE * TILE * F


def layers(
    features, tile_values, tile_columns, tile_present, host_root, host_block,
    self_one, neigh_one, scale_one, shift_one, self_two, neigh_two,
):
    rows = features.reshape(ROOTED, TILE, F)
    scale, shift = scale_one.reshape(1, F), shift_one.reshape(1, F)
    count = features.shape[0] * lax.axis_size(GX_GY_GZ)
    wire = pltpu.HBM((GROUP, TILE, F), bf16)
    split_f32 = pltpu.VMEM((SPLIT, TILE, F), f32)
    view_v = pltpu.VMEM((SLOTS + 1, TILE, F), bf16)
    row_buffer = pltpu.VMEM((HOST, TILE, F), bf16)

    def tile_rows(n):
        return pltpu.VMEM((n, K, TILE, TILE), bf16)

    def exchange(blocks, axes=GZ):
        return lax.all_to_all(blocks, axes, split_axis=0, concat_axis=0, tiled=True)

    def spread(parts):
        column = lax.all_gather(parts, "gz_1", axis=0, tiled=True)
        outgoing = call(
            pass_kernel, 0, 2 << 20,
            out_shape=pltpu.HBM((GROUP,) + parts.shape[1:], bf16),
            in_specs=[SMEM, VMEM],
            out_specs=HBM,
            scratch_shapes=[DMA],
        )(picks, column)
        return exchange(outgoing, "gz_0")

    picks, parts = call(
        begin_kernel, 0, 1 << 18, room=60 << 20,
        out_shape=(pltpu.SMEM((GROUP,), jnp.int32), pltpu.VMEM((SPLIT, TILE, F), bf16)),
        in_specs=[HBM] * 3,
        out_specs=(SMEM, VMEM),
        scratch_shapes=[pltpu.SMEM((GROUP * HOST,), jnp.int32)] * 2 + [DMA((3,))],
    )(host_root, host_block, rows)
    incoming = spread(parts)

    table, view, ready = call(
        tables_kernel, 0, 8 << 20,
        out_shape=(
            pltpu.SMEM((ENTRIES,), jnp.int32),
            view_v,
            tile_rows(READY),
        ),
        in_specs=[SMEM] * 4 + [HBM] * 2,
        out_specs=(SMEM, VMEM, VMEM),
        scratch_shapes=[DMA((2,))],
    )(host_root, host_block, tile_columns, tile_present, rows, tile_values)

    outgoing, view = call(
        replica_kernel, 64 * MAC, 4 << 20,
        out_shape=(wire, view_v),
        in_specs=[SMEM] + [VMEM] * 3 + [HBM],
        out_specs=(HBM, VMEM),
        input_output_aliases={1: 1},
        scratch_shapes=[tile_rows(HOST), row_buffer, DMA, DMA((2,)), DMA],
    )(table, view, incoming, ready, tile_values)
    returned = exchange(outgoing)

    first_own, self_split, part_split, own_sums = call(
        own_kernel, 60 * MAC, 5 << 20,
        out_shape=(pltpu.VMEM((OWN, TILE, F), f32), split_f32, split_f32, pltpu.VMEM((2, F), f32)),
        in_specs=[SMEM, VMEM, HBM, VMEM, VMEM],
        out_specs=(VMEM,) * 4,
        scratch_shapes=[tile_rows(ROOTED), DMA((ROOTED,))],
    )(table, view, tile_values, self_one, neigh_one)

    first_split, sums, parts = call(
        split_kernel, 4 * MAC, 3 << 20,
        out_shape=(
            split_f32,
            pltpu.VMEM((PLANE_SIZE, 2, F), f32),
            pltpu.VMEM((SPLIT, TILE + CENTER_ROWS, F), bf16),
        ),
        in_specs=[SMEM] + [VMEM] * 5,
        out_specs=(VMEM,) * 3,
        scratch_shapes=[pltpu.VMEM((SPLIT, TILE, F), f32)],
    )(table, returned, part_split, self_split, own_sums, neigh_one)
    plane_sums = exchange(sums, PLANE)
    incoming = spread(parts)
    sums = lax.psum(lax.psum(jnp.sum(plane_sums, axis=0), ("gy_0", "gy_1")), "gz_1")

    outgoing, view = call(
        functools.partial(hidden_kernel, count), 64 * MAC, 5 << 20,
        out_shape=(wire, view_v),
        in_specs=[SMEM] + [VMEM] * 6 + [HBM],
        out_specs=(HBM, VMEM),
        scratch_shapes=[tile_rows(HOST), row_buffer, DMA((2,)), DMA],
    )(table, sums, scale, shift, first_own, first_split, incoming, tile_values)
    returned = exchange(outgoing)

    begun, self_split, part_split = call(
        own_two_kernel, 60 * MAC, 5 << 20,
        out_shape=(shape((ROOTED, TILE, F), bf16), split_f32, split_f32),
        in_specs=[SMEM, VMEM, HBM, VMEM, VMEM],
        out_specs=(VMEM,) * 3,
        scratch_shapes=[tile_rows(ROOTED), DMA((ROOTED,))],
    )(table, view, tile_values, self_two, neigh_two)

    embedding = call(
        last_kernel, 4 * MAC, 3 << 20,
        out_shape=shape((ROOTED, TILE, F), bf16),
        in_specs=[SMEM] + [VMEM] * 4 + [ANY],
        out_specs=ANY,
        input_output_aliases={5: 0},
        scratch_shapes=[pltpu.VMEM((SPLIT, TILE, F), f32), pltpu.VMEM((SPLIT, TILE, F), bf16), DMA],
    )(table, returned, part_split, self_split, neigh_two, begun)
    return embedding.reshape(ROOTED * TILE, F)


def solution(mesh):
    finer = Mesh(
        mesh.devices.reshape(mesh.shape["gx"], 2, 2, 4, 4), ("gx", "gy_0", "gy_1", "gz_0", "gz_1")
    )
    return jax.shard_map(
        layers,
        mesh=finer,
        in_specs=(
            P(GX_GY_GZ, None),
            P(GX_GY_GZ, None, None, None),
            P(GX_GY_GZ, None),
            P(GX_GY_GZ, None),
            P(GX_GY),
            P(GX_GY),
            P(),
            P(),
            P(),
            P(),
            P(),
            P(),
        ),
        out_specs=P(GX_GY_GZ, None),
        check_vma=False,
    )
```

```python
import functools

import jax
import jax.numpy as jnp
from jax import lax
from jax.experimental import pallas as pl
from jax.experimental.pallas import tpu as pltpu
from jax.sharding import Mesh
from jax.sharding import PartitionSpec as P

OWN = 4
SPLIT = 2
ROOTED = 6
HOST = 8
SLOTS = 14
K = 8
TILE = 128
F = 256
GROUP = 16
CENTER_ROWS = 16
VMEM_BYTES = 50 << 20
GZ = ("gz_1", "gz_0")
GX_GY_GZ = ("gx", "gy_0", "gy_1", "gz_0", "gz_1")
GX_GY = ("gx", "gy_0", "gy_1")
PLANE = ("gx", "gz_0")
PLANE_SIZE = 32
ROOTS_AT = 112
SEL_AT = 120
TARGETS_AT = 136
ENTRIES = 144
READY = 4
SIDE = 4

f32 = jnp.float32
bf16 = jnp.bfloat16

HBM = pl.BlockSpec(memory_space=pltpu.HBM)
ANY = pl.BlockSpec(memory_space=pl.ANY)
VMEM = pl.BlockSpec(memory_space=pltpu.VMEM)
SMEM = pl.BlockSpec(memory_space=pltpu.SMEM)
DMA = pltpu.SemaphoreType.DMA


def shape(dims, dtype):
    return jax.ShapeDtypeStruct(dims, dtype)


def call(body, flops, size, room=VMEM_BYTES, **kw):
    return pl.pallas_call(
        body,
        compiler_params=pltpu.CompilerParams(vmem_limit_bytes=room),
        cost_estimate=pl.CostEstimate(flops=flops, bytes_accessed=size, transcendentals=0),
        **kw,
    )


def dot(a, b):
    return jnp.dot(a, b, preferred_element_type=f32)


def my_place():
    return lax.axis_index("gz_0") * 4 + lax.axis_index("gz_1")


def swapped(q):
    return (q & (SIDE - 1)) * SIDE + q // SIDE


def loop(n, step):
    lax.fori_loop(0, n, lambda i, c: (step(i), c)[1], 0)


def begin_kernel(root, block, rows, picks, parts, root_s, block_s, sem):
    loads = [
        pltpu.make_async_copy(root, root_s, sem.at[0]),
        pltpu.make_async_copy(block, block_s, sem.at[1]),
        pltpu.make_async_copy(rows.at[pl.ds(OWN, SPLIT)], parts, sem.at[2]),
    ]
    for c in loads:
        c.start()
    for c in loads[:2]:
        c.wait()
    my_x, my_z = lax.axis_index("gz_0"), lax.axis_index("gz_1")

    def pick(i):
        target, source = (i // SIDE) * SIDE + my_z, my_x * SIDE + (i & (SIDE - 1))
        chosen = jnp.int32(0)
        for j in range(HOST):
            at = target * HOST + j
            chosen = jnp.where(root_s[at] == source, block_s[at], chosen)
        picks[i] = chosen

    loop(GROUP, pick)
    loads[2].wait()


def tables_kernel(root, block, cols, present, rows, tiles, table, view, ready, sem):
    load_rows = pltpu.make_async_copy(rows, view.at[pl.ds(0, ROOTED)], sem.at[0])
    load_tiles = pltpu.make_async_copy(tiles.at[pl.ds(ROOTED, READY)], ready, sem.at[1])
    load_rows.start()
    load_tiles.start()
    mine = my_place()

    def select(q):
        held = jnp.int32(0)
        for j in range(HOST):
            held = jnp.where(root[q * HOST + j] == mine, block[q * HOST + j] + 1, held)
        table[SEL_AT + swapped(q)] = held

    def slots(b):
        for k in range(K):
            table[b * K + k] = jnp.where(present[b, k] > 0, cols[b, k], SLOTS)

    loop(SLOTS, slots)
    loop(GROUP, select)
    for h in range(HOST):
        q = root[mine * HOST + h]
        table[ROOTS_AT + h] = q
        table[TARGETS_AT + h] = swapped(q)
    view[SLOTS] = jnp.zeros((TILE, F), bf16)
    load_rows.wait()
    load_tiles.wait()


def tile_copy(tiles, tbuf, tsem, first, i):
    return pltpu.make_async_copy(tiles.at[first + i], tbuf.at[i], tsem.at[i])


def load_tiles(tiles, tbuf, tsem, first, count):
    loop(count, lambda i: tile_copy(tiles, tbuf, tsem, first, i).start())


def tile_sum(table, row_tiles, b, view):
    acc = None
    for k in range(0, K, 2):
        left = jnp.concatenate([row_tiles[k], row_tiles[k + 1]], axis=1)
        right = jnp.concatenate([view[table[b * K + k]], view[table[b * K + k + 1]]], axis=0)
        term = dot(left, right)
        acc = term if acc is None else acc + term
    return acc


def tile_row(table, tiles, tbuf, tsem, i, view):
    tile_copy(tiles, tbuf, tsem, 0, i).wait()
    return tile_sum(table, tbuf.at[i], i, view)


def group_copies(tiles, tbuf, tsem, groups):
    return {
        first: pltpu.make_async_copy(
            tiles.at[pl.ds(ROOTED + first, count)], tbuf.at[pl.ds(first, count)], tsem.at[n]
        )
        for n, (first, count) in enumerate(groups)
    }


def replica_rows(table, row_tiles, waits, out, view, obuf, osem):
    def send(h):
        pltpu.make_async_copy(obuf.at[h], out.at[table[TARGETS_AT + h]], osem).start()

    for h in range(HOST):
        if h in waits:
            waits[h].wait()
        obuf[h] = tile_sum(table, row_tiles(h), ROOTED + h, view).astype(bf16)
        if h:
            send(h - 1)
    send(HOST - 1)
    pltpu.make_async_copy(obuf, out.at[pl.ds(0, HOST)], osem).wait()


def replica_kernel(table, begun, incoming, ready, tiles, out, view, tbuf, obuf, vsem, tsem, osem):
    for h in range(HOST):
        pltpu.make_async_copy(
            incoming.at[table[ROOTS_AT + h]], view.at[ROOTED + h], vsem
        ).start()
    later = group_copies(tiles, tbuf, tsem, ((READY, 2), (READY + 2, 2)))
    for c in later.values():
        c.start()
    pltpu.make_async_copy(
        incoming.at[pl.ds(0, HOST)], view.at[pl.ds(ROOTED, HOST)], vsem
    ).wait()
    replica_rows(
        table, lambda h: ready.at[h] if h < READY else tbuf.at[h], later, out, view, obuf, osem
    )


def own_kernel(table, view, tiles, w_self, w_neigh, first_own, self_split, part_split, sums, tbuf, tsem):
    load_tiles(tiles, tbuf, tsem, 0, ROOTED)
    sums[...] = jnp.zeros((2, F), f32)

    def own(b, carry):
        neighbours = tile_row(table, tiles, tbuf, tsem, b, view).astype(bf16)
        first = dot(view[b], w_self[...]) + dot(neighbours, w_neigh[...])
        first_own[b] = first
        sums[0:1] += jnp.sum(first, axis=0, keepdims=True)
        sums[1:2] += jnp.sum(first * first, axis=0, keepdims=True)
        return carry

    def split(s, carry):
        part_split[s] = tile_row(table, tiles, tbuf, tsem, OWN + s, view)
        self_split[s] = dot(view[OWN + s], w_self[...])
        return carry

    lax.fori_loop(0, OWN, own, 0)
    lax.fori_loop(0, SPLIT, split, 0)


def add_replicas(table, incoming, total):
    def add(q):
        s = table[SEL_AT + q]

        @pl.when(s > 0)
        def _():
            total[s - 1] += incoming[q].astype(f32)

    loop(GROUP, add)


def split_kernel(table, incoming, part_split, self_split, own_sums, w_neigh, first_split, sums, parts, total):
    total[...] = part_split[...]
    add_replicas(table, incoming, total)
    s1, s2 = own_sums[0:1], own_sums[1:2]
    for s in range(SPLIT):
        first = self_split[s] + dot(total[s].astype(bf16), w_neigh[...])
        first_split[s] = first
        s1 += jnp.sum(first, axis=0, keepdims=True)
        s2 += jnp.sum(first * first, axis=0, keepdims=True)

    def fill(q):
        sums[q, 0:1] = s1
        sums[q, 1:2] = s2

    loop(PLANE_SIZE, fill)
    center = (s1 * (1.0 / (ROOTED * TILE))).astype(bf16)
    less = center.astype(f32)
    for s in range(SPLIT):
        parts[s, pl.ds(0, TILE)] = (first_split[s] - less).astype(bf16)
        parts[s, pl.ds(TILE, CENTER_ROWS)] = jnp.broadcast_to(center, (CENTER_ROWS, F))


def pass_kernel(picks, column, out, sem):
    def send(i):
        chosen = (i & (SIDE - 1)) * SPLIT + picks[i]
        return pltpu.make_async_copy(column.at[chosen], out.at[i], sem)

    loop(GROUP, lambda i: send(i).start())
    pltpu.make_async_copy(out, out, sem).wait()


def hidden_kernel(
    count, table, sums, scale, shift, first_own, first_split, incoming, tiles,
    out, view, tbuf, obuf, tsem, osem,
):
    copies = group_copies(tiles, tbuf, tsem, ((0, 4), (4, 4)))
    for c in copies.values():
        c.start()
    mean = sums[0:1] * (1.0 / count)
    var = sums[1:2] * (1.0 / count) - mean * mean
    inv = lax.rsqrt(var + 1e-5)

    def norm(first, less):
        return jax.nn.relu((first - less) * inv * scale[...] + shift[...]).astype(bf16)

    def own(b, carry):
        view[b] = norm(first_own[b], mean)
        return carry

    def split(s, carry):
        view[OWN + s] = norm(first_split[s], mean)
        return carry

    def hosted(h, carry):
        q = table[ROOTS_AT + h]
        centered = incoming[q, pl.ds(0, TILE)].astype(f32)
        center = incoming[q, pl.ds(TILE, CENTER_ROWS)].astype(f32)[0:1]
        view[ROOTED + h] = norm(centered, mean - center)
        return carry

    lax.fori_loop(0, OWN, own, 0)
    lax.fori_loop(0, SPLIT, split, 0)
    lax.fori_loop(0, HOST, hosted, 0)
    view[SLOTS] = jnp.zeros((TILE, F), bf16)
    replica_rows(table, lambda h: tbuf.at[h], copies, out, view, obuf, osem)


def own_two_kernel(table, view, tiles, w_self, w_neigh, out, self_split, part_split, tbuf, tsem):
    load_tiles(tiles, tbuf, tsem, 0, ROOTED)

    def own(b, carry):
        neighbours = tile_row(table, tiles, tbuf, tsem, b, view).astype(bf16)
        second = dot(view[b], w_self[...]) + dot(neighbours, w_neigh[...])
        out[b] = second.astype(bf16)
        return carry

    def split(s, carry):
        part_split[s] = tile_row(table, tiles, tbuf, tsem, OWN + s, view)
        self_split[s] = dot(view[OWN + s], w_self[...])
        return carry

    lax.fori_loop(0, OWN, own, 0)
    lax.fori_loop(0, SPLIT, split, 0)


def last_kernel(table, incoming, part_split, self_split, w_neigh, begun, out, total, done, sem):
    total[...] = part_split[...]
    add_replicas(table, incoming, total)
    for s in range(SPLIT):
        done[s] = (self_split[s] + dot(total[s].astype(bf16), w_neigh[...])).astype(bf16)
    put = pltpu.make_async_copy(done, out.at[pl.ds(OWN, SPLIT)], sem)
    put.start()
    put.wait()


MAC = 2 * TILE * TILE * F


def layers(
    features, tile_values, tile_columns, tile_present, host_root, host_block,
    self_one, neigh_one, scale_one, shift_one, self_two, neigh_two,
):
    rows = features.reshape(ROOTED, TILE, F)
    scale, shift = scale_one.reshape(1, F), shift_one.reshape(1, F)
    count = features.shape[0] * lax.axis_size(GX_GY_GZ)
    wire = pltpu.HBM((GROUP, TILE, F), bf16)
    split_f32 = pltpu.VMEM((SPLIT, TILE, F), f32)
    view_v = pltpu.VMEM((SLOTS + 1, TILE, F), bf16)
    row_buffer = pltpu.VMEM((HOST, TILE, F), bf16)

    def tile_rows(n):
        return pltpu.VMEM((n, K, TILE, TILE), bf16)

    def exchange(blocks, axes=GZ):
        return lax.all_to_all(blocks, axes, split_axis=0, concat_axis=0, tiled=True)

    def spread(parts):
        column = lax.all_gather(parts, "gz_1", axis=0, tiled=True)
        outgoing = call(
            pass_kernel, 0, 2 << 20,
            out_shape=pltpu.HBM((GROUP,) + parts.shape[1:], bf16),
            in_specs=[SMEM, VMEM],
            out_specs=HBM,
            scratch_shapes=[DMA],
        )(picks, column)
        return exchange(outgoing, "gz_0")

    picks, parts = call(
        begin_kernel, 0, 1 << 18, room=60 << 20,
        out_shape=(pltpu.SMEM((GROUP,), jnp.int32), pltpu.VMEM((SPLIT, TILE, F), bf16)),
        in_specs=[HBM] * 3,
        out_specs=(SMEM, VMEM),
        scratch_shapes=[pltpu.SMEM((GROUP * HOST,), jnp.int32)] * 2 + [DMA((3,))],
    )(host_root, host_block, rows)
    incoming = spread(parts)

    table, view, ready = call(
        tables_kernel, 0, 8 << 20,
        out_shape=(
            pltpu.SMEM((ENTRIES,), jnp.int32),
            view_v,
            tile_rows(READY),
        ),
        in_specs=[SMEM] * 4 + [HBM] * 2,
        out_specs=(SMEM, VMEM, VMEM),
        scratch_shapes=[DMA((2,))],
    )(host_root, host_block, tile_columns, tile_present, rows, tile_values)

    outgoing, view = call(
        replica_kernel, 64 * MAC, 4 << 20,
        out_shape=(wire, view_v),
        in_specs=[SMEM] + [VMEM] * 3 + [HBM],
        out_specs=(HBM, VMEM),
        input_output_aliases={1: 1},
        scratch_shapes=[tile_rows(HOST), row_buffer, DMA, DMA((2,)), DMA],
    )(table, view, incoming, ready, tile_values)
    returned = exchange(outgoing)

    first_own, self_split, part_split, own_sums = call(
        own_kernel, 60 * MAC, 5 << 20,
        out_shape=(pltpu.VMEM((OWN, TILE, F), f32), split_f32, split_f32, pltpu.VMEM((2, F), f32)),
        in_specs=[SMEM, VMEM, HBM, VMEM, VMEM],
        out_specs=(VMEM,) * 4,
        scratch_shapes=[tile_rows(ROOTED), DMA((ROOTED,))],
    )(table, view, tile_values, self_one, neigh_one)

    first_split, sums, parts = call(
        split_kernel, 4 * MAC, 3 << 20,
        out_shape=(
            split_f32,
            pltpu.VMEM((PLANE_SIZE, 2, F), f32),
            pltpu.VMEM((SPLIT, TILE + CENTER_ROWS, F), bf16),
        ),
        in_specs=[SMEM] + [VMEM] * 5,
        out_specs=(VMEM,) * 3,
        scratch_shapes=[pltpu.VMEM((SPLIT, TILE, F), f32)],
    )(table, returned, part_split, self_split, own_sums, neigh_one)
    plane_sums = exchange(sums, PLANE)
    incoming = spread(parts)
    sums = lax.psum(lax.psum(jnp.sum(plane_sums, axis=0), ("gy_0", "gy_1")), "gz_1")

    outgoing, view = call(
        functools.partial(hidden_kernel, count), 64 * MAC, 5 << 20,
        out_shape=(wire, view_v),
        in_specs=[SMEM] + [VMEM] * 6 + [HBM],
        out_specs=(HBM, VMEM),
        scratch_shapes=[tile_rows(HOST), row_buffer, DMA((2,)), DMA],
    )(table, sums, scale, shift, first_own, first_split, incoming, tile_values)
    returned = exchange(outgoing)

    begun, self_split, part_split = call(
        own_two_kernel, 60 * MAC, 5 << 20,
        out_shape=(shape((ROOTED, TILE, F), bf16), split_f32, split_f32),
        in_specs=[SMEM, VMEM, HBM, VMEM, VMEM],
        out_specs=(VMEM,) * 3,
        scratch_shapes=[tile_rows(ROOTED), DMA((ROOTED,))],
    )(table, view, tile_values, self_two, neigh_two)

    embedding = call(
        last_kernel, 4 * MAC, 3 << 20,
        out_shape=shape((ROOTED, TILE, F), bf16),
        in_specs=[SMEM] + [VMEM] * 4 + [ANY],
        out_specs=ANY,
        input_output_aliases={5: 0},
        scratch_shapes=[pltpu.VMEM((SPLIT, TILE, F), f32), pltpu.VMEM((SPLIT, TILE, F), bf16), DMA],
    )(table, returned, part_split, self_split, neigh_two, begun)
    return embedding.reshape(ROOTED * TILE, F)


def solution(mesh):
    finer = Mesh(
        mesh.devices.reshape(mesh.shape["gx"], 2, 2, 4, 4), ("gx", "gy_0", "gy_1", "gz_0", "gz_1")
    )
    return jax.shard_map(
        layers,
        mesh=finer,
        in_specs=(
            P(GX_GY_GZ, None),
            P(GX_GY_GZ, None, None, None),
            P(GX_GY_GZ, None),
            P(GX_GY_GZ, None),
            P(GX_GY),
            P(GX_GY),
            P(),
            P(),
            P(),
            P(),
            P(),
            P(),
        ),
        out_specs=P(GX_GY_GZ, None),
        check_vma=False,
    )
```

```python
import functools

import jax
import jax.numpy as jnp
from jax import lax
from jax.experimental import pallas as pl
from jax.experimental.pallas import tpu as pltpu
from jax.sharding import Mesh
from jax.sharding import PartitionSpec as P

OWN = 4
SPLIT = 2
ROOTED = 6
HOST = 8
SLOTS = 14
K = 8
TILE = 128
F = 256
GROUP = 16
CENTER_ROWS = 16
VMEM_BYTES = 50 << 20
GZ = ("gz_0", "gz_1")
GX_GY_GZ = ("gx", "gy_0", "gy_1", "gz_0", "gz_1")
GX_GY = ("gx", "gy_0", "gy_1")
PLANE = ("gx", "gz_0")
PLANE_SIZE = 32
ROOTS_AT = 112
SEL_AT = 120
ENTRIES = 136
READY = 4
SIDE = 4

f32 = jnp.float32
bf16 = jnp.bfloat16

HBM = pl.BlockSpec(memory_space=pltpu.HBM)
ANY = pl.BlockSpec(memory_space=pl.ANY)
VMEM = pl.BlockSpec(memory_space=pltpu.VMEM)
SMEM = pl.BlockSpec(memory_space=pltpu.SMEM)
DMA = pltpu.SemaphoreType.DMA


def shape(dims, dtype):
    return jax.ShapeDtypeStruct(dims, dtype)


def call(body, flops, size, room=VMEM_BYTES, **kw):
    return pl.pallas_call(
        body,
        compiler_params=pltpu.CompilerParams(vmem_limit_bytes=room),
        cost_estimate=pl.CostEstimate(flops=flops, bytes_accessed=size, transcendentals=0),
        **kw,
    )


def dot(a, b):
    return jnp.dot(a, b, preferred_element_type=f32)


def my_place():
    return lax.axis_index("gz_0") * 4 + lax.axis_index("gz_1")


def loop(n, step):
    lax.fori_loop(0, n, lambda i, c: (step(i), c)[1], 0)


def begin_kernel(root, block, rows, picks, parts, root_s, block_s, sem):
    loads = [
        pltpu.make_async_copy(root, root_s, sem.at[0]),
        pltpu.make_async_copy(block, block_s, sem.at[1]),
        pltpu.make_async_copy(rows.at[pl.ds(OWN, SPLIT)], parts, sem.at[2]),
    ]
    for c in loads:
        c.start()
    for c in loads[:2]:
        c.wait()
    my_x, my_z = lax.axis_index("gz_0"), lax.axis_index("gz_1")

    def pick(i):
        target, source = (i // SIDE) * SIDE + my_z, my_x * SIDE + (i & (SIDE - 1))
        chosen = jnp.int32(0)
        for j in range(HOST):
            at = target * HOST + j
            chosen = jnp.where(root_s[at] == source, block_s[at], chosen)
        picks[i] = chosen

    loop(GROUP, pick)
    loads[2].wait()


def tables_kernel(root, block, cols, present, rows, tiles, table, view, ready, sem):
    load_rows = pltpu.make_async_copy(rows, view.at[pl.ds(0, ROOTED)], sem.at[0])
    load_tiles = pltpu.make_async_copy(tiles.at[pl.ds(ROOTED, READY)], ready, sem.at[1])
    load_rows.start()
    load_tiles.start()
    mine = my_place()

    def select(q):
        held = jnp.int32(0)
        for j in range(HOST):
            held = jnp.where(root[q * HOST + j] == mine, block[q * HOST + j] + 1, held)
        table[SEL_AT + q] = held

    def slots(b):
        for k in range(K):
            table[b * K + k] = jnp.where(present[b, k] > 0, cols[b, k], SLOTS)

    loop(SLOTS, slots)
    loop(GROUP, select)
    for h in range(HOST):
        table[ROOTS_AT + h] = root[mine * HOST + h]
    view[SLOTS] = jnp.zeros((TILE, F), bf16)
    load_rows.wait()
    load_tiles.wait()


def tile_copy(tiles, tbuf, tsem, first, i):
    return pltpu.make_async_copy(tiles.at[first + i], tbuf.at[i], tsem.at[i])


def load_tiles(tiles, tbuf, tsem, first, count):
    loop(count, lambda i: tile_copy(tiles, tbuf, tsem, first, i).start())


def tile_sum(table, row_tiles, b, view):
    acc = None
    for k in range(0, K, 2):
        left = jnp.concatenate([row_tiles[k], row_tiles[k + 1]], axis=1)
        right = jnp.concatenate([view[table[b * K + k]], view[table[b * K + k + 1]]], axis=0)
        term = dot(left, right)
        acc = term if acc is None else acc + term
    return acc


def tile_row(table, tiles, tbuf, tsem, i, view):
    tile_copy(tiles, tbuf, tsem, 0, i).wait()
    return tile_sum(table, tbuf.at[i], i, view)


def group_copies(tiles, tbuf, tsem, groups):
    return {
        first: pltpu.make_async_copy(
            tiles.at[pl.ds(ROOTED + first, count)], tbuf.at[pl.ds(first, count)], tsem.at[n]
        )
        for n, (first, count) in enumerate(groups)
    }


def replica_rows(table, row_tiles, waits, out, view, obuf, osem):
    def send(h):
        pltpu.make_async_copy(obuf.at[h], out.at[table[ROOTS_AT + h]], osem).start()

    for h in range(HOST):
        if h in waits:
            waits[h].wait()
        obuf[h] = tile_sum(table, row_tiles(h), ROOTED + h, view).astype(bf16)
        if h:
            send(h - 1)
    send(HOST - 1)
    pltpu.make_async_copy(obuf, out.at[pl.ds(0, HOST)], osem).wait()


def replica_kernel(table, begun, incoming, ready, tiles, out, view, tbuf, obuf, vsem, tsem, osem):
    for h in range(HOST):
        pltpu.make_async_copy(
            incoming.at[table[ROOTS_AT + h]], view.at[ROOTED + h], vsem
        ).start()
    later = group_copies(tiles, tbuf, tsem, ((READY, 2), (READY + 2, 2)))
    for c in later.values():
        c.start()
    pltpu.make_async_copy(
        incoming.at[pl.ds(0, HOST)], view.at[pl.ds(ROOTED, HOST)], vsem
    ).wait()
    replica_rows(
        table, lambda h: ready.at[h] if h < READY else tbuf.at[h], later, out, view, obuf, osem
    )


def own_kernel(table, view, tiles, w_self, w_neigh, first_own, self_split, part_split, sums, tbuf, tsem):
    load_tiles(tiles, tbuf, tsem, 0, ROOTED)
    sums[...] = jnp.zeros((2, F), f32)

    def own(b, carry):
        neighbours = tile_row(table, tiles, tbuf, tsem, b, view).astype(bf16)
        first = dot(view[b], w_self[...]) + dot(neighbours, w_neigh[...])
        first_own[b] = first
        sums[0:1] += jnp.sum(first, axis=0, keepdims=True)
        sums[1:2] += jnp.sum(first * first, axis=0, keepdims=True)
        return carry

    def split(s, carry):
        part_split[s] = tile_row(table, tiles, tbuf, tsem, OWN + s, view)
        self_split[s] = dot(view[OWN + s], w_self[...])
        return carry

    lax.fori_loop(0, OWN, own, 0)
    lax.fori_loop(0, SPLIT, split, 0)


def add_replicas(table, incoming, total):
    def add(q):
        s = table[SEL_AT + q]

        @pl.when(s > 0)
        def _():
            total[s - 1] += incoming[q].astype(f32)

    loop(GROUP, add)


def split_kernel(table, incoming, part_split, self_split, own_sums, w_neigh, first_split, sums, parts, total):
    total[...] = part_split[...]
    add_replicas(table, incoming, total)
    s1, s2 = own_sums[0:1], own_sums[1:2]
    for s in range(SPLIT):
        first = self_split[s] + dot(total[s].astype(bf16), w_neigh[...])
        first_split[s] = first
        s1 += jnp.sum(first, axis=0, keepdims=True)
        s2 += jnp.sum(first * first, axis=0, keepdims=True)

    def fill(q):
        sums[q, 0:1] = s1
        sums[q, 1:2] = s2

    loop(PLANE_SIZE, fill)
    center = (s1 * (1.0 / (ROOTED * TILE))).astype(bf16)
    less = center.astype(f32)
    for s in range(SPLIT):
        parts[s, pl.ds(0, TILE)] = (first_split[s] - less).astype(bf16)
        parts[s, pl.ds(TILE, CENTER_ROWS)] = jnp.broadcast_to(center, (CENTER_ROWS, F))


def send_picked(picks, column, out, sem):
    def send(i):
        chosen = (i & (SIDE - 1)) * SPLIT + picks[i]
        pltpu.make_async_copy(column.at[chosen], out.at[i], sem).start()

    loop(GROUP, send)


def pass_kernel(picks, column, out, sem):
    send_picked(picks, column, out, sem)
    pltpu.make_async_copy(out, out, sem).wait()


def pass_and_sum_kernel(picks, column, plane_sums, out, sums, sem):
    send_picked(picks, column, out, sem)
    sums[...] = jnp.sum(plane_sums[...], axis=0)
    pltpu.make_async_copy(out, out, sem).wait()


def hidden_kernel(
    count, table, sums, scale, shift, first_own, first_split, incoming, tiles,
    out, view, tbuf, obuf, tsem, osem,
):
    copies = group_copies(tiles, tbuf, tsem, ((0, 4), (4, 4)))
    for c in copies.values():
        c.start()
    mean = sums[0:1] * (1.0 / count)
    var = sums[1:2] * (1.0 / count) - mean * mean
    inv = lax.rsqrt(var + 1e-5)

    def norm(first, less):
        return jax.nn.relu((first - less) * inv * scale[...] + shift[...]).astype(bf16)

    def own(b, carry):
        view[b] = norm(first_own[b], mean)
        return carry

    def split(s, carry):
        view[OWN + s] = norm(first_split[s], mean)
        return carry

    def hosted(h, carry):
        q = table[ROOTS_AT + h]
        centered = incoming[q, pl.ds(0, TILE)].astype(f32)
        center = incoming[q, pl.ds(TILE, CENTER_ROWS)].astype(f32)[0:1]
        view[ROOTED + h] = norm(centered, mean - center)
        return carry

    lax.fori_loop(0, OWN, own, 0)
    lax.fori_loop(0, SPLIT, split, 0)
    lax.fori_loop(0, HOST, hosted, 0)
    view[SLOTS] = jnp.zeros((TILE, F), bf16)
    replica_rows(table, lambda h: tbuf.at[h], copies, out, view, obuf, osem)


def own_two_kernel(table, view, tiles, w_self, w_neigh, out, self_split, part_split, tbuf, tsem):
    load_tiles(tiles, tbuf, tsem, 0, ROOTED)

    def own(b, carry):
        neighbours = tile_row(table, tiles, tbuf, tsem, b, view).astype(bf16)
        second = dot(view[b], w_self[...]) + dot(neighbours, w_neigh[...])
        out[b] = second.astype(bf16)
        return carry

    def split(s, carry):
        part_split[s] = tile_row(table, tiles, tbuf, tsem, OWN + s, view)
        self_split[s] = dot(view[OWN + s], w_self[...])
        return carry

    lax.fori_loop(0, OWN, own, 0)
    lax.fori_loop(0, SPLIT, split, 0)


def last_kernel(table, incoming, part_split, self_split, w_neigh, begun, out, total, done, sem):
    total[...] = part_split[...]
    add_replicas(table, incoming, total)
    for s in range(SPLIT):
        done[s] = (self_split[s] + dot(total[s].astype(bf16), w_neigh[...])).astype(bf16)
    put = pltpu.make_async_copy(done, out.at[pl.ds(OWN, SPLIT)], sem)
    put.start()
    put.wait()


MAC = 2 * TILE * TILE * F


def layers(
    features, tile_values, tile_columns, tile_present, host_root, host_block,
    self_one, neigh_one, scale_one, shift_one, self_two, neigh_two,
):
    rows = features.reshape(ROOTED, TILE, F)
    scale, shift = scale_one.reshape(1, F), shift_one.reshape(1, F)
    count = features.shape[0] * lax.axis_size(GX_GY_GZ)
    wire = pltpu.HBM((GROUP, TILE, F), bf16)
    split_f32 = pltpu.VMEM((SPLIT, TILE, F), f32)
    view_v = pltpu.VMEM((SLOTS + 1, TILE, F), bf16)
    row_buffer = pltpu.VMEM((HOST, TILE, F), bf16)

    def tile_rows(n):
        return pltpu.VMEM((n, K, TILE, TILE), bf16)

    def exchange(blocks, axes=GZ):
        return lax.all_to_all(blocks, axes, split_axis=0, concat_axis=0, tiled=True)

    def gather(parts):
        return lax.all_gather(parts, "gz_1", axis=0, tiled=True)

    picks, parts = call(
        begin_kernel, 0, 1 << 18, room=60 << 20,
        out_shape=(pltpu.SMEM((GROUP,), jnp.int32), pltpu.VMEM((SPLIT, TILE, F), bf16)),
        in_specs=[HBM] * 3,
        out_specs=(SMEM, VMEM),
        scratch_shapes=[pltpu.SMEM((GROUP * HOST,), jnp.int32)] * 2 + [DMA((3,))],
    )(host_root, host_block, rows)
    outgoing = call(
        pass_kernel, 0, 2 << 20,
        out_shape=wire,
        in_specs=[SMEM, VMEM],
        out_specs=HBM,
        scratch_shapes=[DMA],
    )(picks, gather(parts))
    incoming = exchange(outgoing, "gz_0")

    table, view, ready = call(
        tables_kernel, 0, 8 << 20,
        out_shape=(
            pltpu.SMEM((ENTRIES,), jnp.int32),
            view_v,
            tile_rows(READY),
        ),
        in_specs=[SMEM] * 4 + [HBM] * 2,
        out_specs=(SMEM, VMEM, VMEM),
        scratch_shapes=[DMA((2,))],
    )(host_root, host_block, tile_columns, tile_present, rows, tile_values)

    outgoing, view = call(
        replica_kernel, 64 * MAC, 4 << 20,
        out_shape=(wire, view_v),
        in_specs=[SMEM] + [VMEM] * 3 + [HBM],
        out_specs=(HBM, VMEM),
        input_output_aliases={1: 1},
        scratch_shapes=[tile_rows(HOST), row_buffer, DMA, DMA((2,)), DMA],
    )(table, view, incoming, ready, tile_values)
    returned = exchange(outgoing)

    first_own, self_split, part_split, own_sums = call(
        own_kernel, 60 * MAC, 5 << 20,
        out_shape=(pltpu.VMEM((OWN, TILE, F), f32), split_f32, split_f32, pltpu.VMEM((2, F), f32)),
        in_specs=[SMEM, VMEM, HBM, VMEM, VMEM],
        out_specs=(VMEM,) * 4,
        scratch_shapes=[tile_rows(ROOTED), DMA((ROOTED,))],
    )(table, view, tile_values, self_one, neigh_one)

    first_split, sums, parts = call(
        split_kernel, 4 * MAC, 3 << 20,
        out_shape=(
            split_f32,
            pltpu.VMEM((PLANE_SIZE, 2, F), f32),
            pltpu.VMEM((SPLIT, TILE + CENTER_ROWS, F), bf16),
        ),
        in_specs=[SMEM] + [VMEM] * 5,
        out_specs=(VMEM,) * 3,
        scratch_shapes=[pltpu.VMEM((SPLIT, TILE, F), f32)],
    )(table, returned, part_split, self_split, own_sums, neigh_one)
    plane_sums = exchange(sums, PLANE)
    column = gather(parts)
    outgoing, sums = call(
        pass_and_sum_kernel, 0, 2 << 20,
        out_shape=(
            pltpu.HBM((GROUP, TILE + CENTER_ROWS, F), bf16),
            pltpu.VMEM((2, F), f32),
        ),
        in_specs=[SMEM, VMEM, VMEM],
        out_specs=(HBM, VMEM),
        scratch_shapes=[DMA],
    )(picks, column, plane_sums)
    incoming = exchange(outgoing, "gz_0")
    sums = lax.psum(lax.psum(sums, ("gy_0", "gy_1")), "gz_1")

    outgoing, view = call(
        functools.partial(hidden_kernel, count), 64 * MAC, 5 << 20,
        out_shape=(wire, view_v),
        in_specs=[SMEM] + [VMEM] * 6 + [HBM],
        out_specs=(HBM, VMEM),
        scratch_shapes=[tile_rows(HOST), row_buffer, DMA((2,)), DMA],
    )(table, sums, scale, shift, first_own, first_split, incoming, tile_values)
    returned = exchange(outgoing)

    begun, self_split, part_split = call(
        own_two_kernel, 60 * MAC, 5 << 20,
        out_shape=(shape((ROOTED, TILE, F), bf16), split_f32, split_f32),
        in_specs=[SMEM, VMEM, HBM, VMEM, VMEM],
        out_specs=(VMEM,) * 3,
        scratch_shapes=[tile_rows(ROOTED), DMA((ROOTED,))],
    )(table, view, tile_values, self_two, neigh_two)

    embedding = call(
        last_kernel, 4 * MAC, 3 << 20,
        out_shape=shape((ROOTED, TILE, F), bf16),
        in_specs=[SMEM] + [VMEM] * 4 + [ANY],
        out_specs=ANY,
        input_output_aliases={5: 0},
        scratch_shapes=[pltpu.VMEM((SPLIT, TILE, F), f32), pltpu.VMEM((SPLIT, TILE, F), bf16), DMA],
    )(table, returned, part_split, self_split, neigh_two, begun)
    return embedding.reshape(ROOTED * TILE, F)


def solution(mesh):
    finer = Mesh(
        mesh.devices.reshape(mesh.shape["gx"], 2, 2, 4, 4), ("gx", "gy_0", "gy_1", "gz_0", "gz_1")
    )
    return jax.shard_map(
        layers,
        mesh=finer,
        in_specs=(
            P(GX_GY_GZ, None),
            P(GX_GY_GZ, None, None, None),
            P(GX_GY_GZ, None),
            P(GX_GY_GZ, None),
            P(GX_GY),
            P(GX_GY),
            P(),
            P(),
            P(),
            P(),
            P(),
            P(),
        ),
        out_specs=P(GX_GY_GZ, None),
        check_vma=False,
    )
```
